256 devices in a mesh: tiles: 64 (over z, x, core), views: 4 (over y).
Axes of the slice: x: 4, y: 4, z: 8, core: 2. Of those that a mesh axis runs over, the one named last changes fastest.
Arguments:
- ref_features: bfloat16 [64, 8, 4096], P('tiles'), may hold values from -6 to 6
- partner_lines: bfloat16 [64, 4, 8, 8192], P('tiles'), may hold values from -6 to 6
- line_owner: int32 [64, 32, 1], P('tiles'), may hold values from 0 to 63; in each aligned block of 32 rows (0 to 31, 32 to 63, ..., all dimensions but the last counted through in order) at most 2 rows name the same one
- line_index: int32 [64, 32], P('tiles'), may hold values from 0 to 7
- line_offset: int32 [64, 32], P('tiles'), may hold values from 0 to 64
- neighbours: int32 [64, 4], replicated, may hold values from -1 to 63, as said below
- conv1_weight: bfloat16 [3, 3, 3, 8, 32], replicated, may hold values from -0.4375 to 0.4375
- conv1_bias: float32 [32], replicated, may hold values from -3 to 3
- conv2_weight: bfloat16 [3, 3, 3, 32, 32], replicated, may hold values from -0.21875 to 0.21875
- conv2_bias: float32 [32], replicated, may hold values from -3 to 3
Outputs:
- regularized: float32 [64, 64, 8, 4096], P('tiles', 'views')
The draws below stay inside these ranges and needn't reach their ends.
Inputs may be any that keep to these rules, and one draw needn't show every extreme that they name: `line_owner`: among the 32 requests of one tile (aligned blocks of rows), no owner is named more than 2 times. Tile positions in a grid of 16 rows and 4 columns are a permutation of the tiles; neighbours lists the tiles above, below, left and right, -1 at the grid's edge.
All inputs are finite; a program needn't handle non-finite values.
Results may differ from the reference program's by a relative error of at most 0.0019.
Values may be sent and summed in bfloat16 or wider, within the bound.
No kernel may reach another device: no remote copies, remote signals or barrier semaphores. Data moves between devices by JAX's collectives and lax.ppermute only.
A program may use at most 128 MiB of HBM per device.

```python
import math
import jax
import jax.numpy as jnp
import numpy as np
from jax import lax

C = 32
G = 8
CH = 32
NDISP = 64
W = 128
SW = 256
NPV = 4
H = 8
MCOLS = 4
TILES = 64
NREQ = 32
CAP = 2


def draw_neighbours(key, part):
    placed = jax.random.permutation(key, TILES).astype(jnp.int32)
    positions = jnp.arange(TILES, dtype=jnp.int32)
    grid_row = positions // MCOLS
    grid_col = positions % MCOLS
    grid_height = TILES // MCOLS

    def tile_at(row_at, col_at, inside):
        spot = jnp.clip(row_at, 0, grid_height - 1) * MCOLS + jnp.clip(col_at, 0, MCOLS - 1)
        return jnp.where(inside, placed[spot], -1)
    links = jnp.stack([tile_at(grid_row - 1, grid_col, grid_row > 0), tile_at(grid_row + 1, grid_col, grid_row < grid_height - 1), tile_at(grid_row, grid_col - 1, grid_col > 0), tile_at(grid_row, grid_col + 1, grid_col < MCOLS - 1)], axis=1).astype(jnp.int32)
    return jnp.zeros((TILES, 4), jnp.int32).at[placed].set(links)


def set_ends(drawn, key, low, high):
    extent = drawn.shape
    spot = [jax.random.randint(jax.random.fold_in(key, axis), (), 0, extent[axis]) for axis in range(len(extent))]
    drawn = drawn.at[tuple(spot)].set(low)
    longest = extent.index(max(extent))
    spot[longest] = (spot[longest] + 1) % extent[longest]
    return drawn.at[tuple(spot)].set(high)


def level_of(own_key, dims, pieces, smallest, top_value):
    level, own = 1.0, jax.random.fold_in(own_key, 6)
    for position, parts in pieces:
        heights = jnp.exp(jax.random.uniform(jax.random.fold_in(own, position), (parts,), jnp.float32, smallest / len(pieces), top_value / len(pieces)))
        level = level * jnp.repeat(heights, dims[position] // parts).reshape([-1 if axis == position else 1 for axis in range(len(dims))])
    return level


def deal_out(stream_key, own, number, rows, count, top, limit, slope):
    sequence = jax.random.permutation(stream_key, count)
    heavy_load, usual = load_shares(count, rows * top, limit, slope, True), load_shares(count, rows * top, limit, slope, False)
    places = jnp.arange(count)

    def named(sizes, rotation):
        used = int((sizes > 0).sum())
        fixed = max(1, used // 4)
        moved = fixed + (places - fixed + rotation * (used - fixed)) % max(1, count - fixed)
        return jnp.zeros((count,), jnp.int32).at[sequence[jnp.where(places < fixed, places, moved)]].set(jnp.asarray(sizes, jnp.int32))

    sizes = jnp.where(number % 4 == 0, named(heavy_load, number // 4), named(usual, number - number // 4 - 1))
    mixed = jax.random.permutation(jax.random.fold_in(own, 3), count)
    giver, taker = mixed[0:count // 2 * 2:2], mixed[1:count // 2 * 2:2]
    room = jnp.minimum(sizes[giver] - 1, limit - sizes[taker]) // 2
    room = jnp.where((giver == sequence[0]) | (taker == sequence[0]) | (sizes[taker] == 0), 0, jnp.maximum(room, 0))
    moved = jax.random.randint(jax.random.fold_in(own, 4), (count // 2,), 0, 1 << 20) % (room + 1)
    sizes = sizes.at[giver].add(-moved).at[taker].add(moved)
    labels = jnp.searchsorted(jnp.cumsum(sizes), jnp.arange(rows * top), side="right").astype(jnp.int32)
    grid = labels.reshape(top, rows).T
    grid = grid[jax.random.permutation(jax.random.fold_in(own, 1), rows)]
    rotation = jax.random.randint(jax.random.fold_in(own, 2), (rows, 1), 0, top)
    return jnp.take_along_axis(grid, (jnp.arange(top)[None, :] + rotation) % top, axis=1)


def load_shares(count, total, limit, lean, full):
    portions = [(1 << 20) // math.isqrt(grade ** lean) + 1 for grade in range(1, count + 1)]
    largest = limit if full else min(limit, max(-(-total // count), total * portions[0] // sum(portions)))
    least = 1 if total - largest >= count - 1 else 0
    holding, rest = [largest] + [least] * (count - 1), total - largest - least * (count - 1)
    while rest > 0:
        candidates = [i for i in range(1, count) if holding[i] < largest] or [i for i in range(1, count) if holding[i] < limit]
        mass, budget = sum([portions[i] for i in candidates]), rest
        for i in candidates:
            more = min(limit - holding[i], max(1, budget * portions[i] // mass), rest)
            holding[i] = holding[i] + more
            rest = rest - more
    return np.array(holding)


def scatter_about(key, extent, width, limit, cuts=(), held_as=jnp.bfloat16):
    factor_of = level_of(key, extent, cuts, -0.22, 0.18) if cuts else 1.0
    entries = jax.random.normal(key, extent, jnp.float32) * width * factor_of
    return jnp.minimum(jnp.maximum(entries, -limit), limit).astype(held_as)


def setup_inputs(seed: int = 0) -> dict:
    key_of = jax.random.split(jax.random.key(seed), 11)
    ref_features = scatter_about(key_of[0], (TILES, H, W * C), 1.0, 6.0, ((0, 64),))
    partner_lines = scatter_about(key_of[1], (TILES, NPV, H, SW * C), 1.0, 6.0, ((0, 64),))
    line_owner_keys = jax.random.split(jax.random.fold_in(key_of[2], 1), TILES * NREQ // NREQ)
    line_owner_turns = jax.random.permutation(jax.random.fold_in(key_of[2], 3), TILES * NREQ // NREQ)
    line_owner = jax.vmap(lambda own, number: deal_out(jax.random.fold_in(key_of[2], 2), own, number, NREQ, TILES, 1, CAP, 2))(line_owner_keys, line_owner_turns).reshape((TILES, NREQ, 1))
    line_index = set_ends(jax.random.randint(key_of[3], (TILES, NREQ), 0, H), jax.random.fold_in(key_of[3], 1), 0, H - 1).astype(jnp.int32)
    line_offset = set_ends(jax.random.randint(key_of[4], (TILES, NREQ), 0, SW - W - NDISP + 1), jax.random.fold_in(key_of[4], 1), 0, SW - W - NDISP).astype(jnp.int32)
    neighbours = draw_neighbours(jax.random.fold_in(key_of[10], 71), 0)
    conv1_weight = scatter_about(key_of[6], (3, 3, 3, G, CH), (27 * G) ** -0.5, 0.4375)
    conv1_bias = scatter_about(key_of[7], (CH,), 0.5, 3.0, (), jnp.float32)
    conv2_weight = scatter_about(key_of[8], (3, 3, 3, CH, CH), (27 * CH) ** -0.5, 0.21875)
    conv2_bias = scatter_about(key_of[9], (CH,), 0.5, 3.0, (), jnp.float32)
    return {"ref_features": ref_features, "partner_lines": partner_lines, "line_owner": line_owner, "line_index": line_index, "line_offset": line_offset, "neighbours": neighbours, "conv1_weight": conv1_weight, "conv1_bias": conv1_bias, "conv2_weight": conv2_weight, "conv2_bias": conv2_bias}


def pick_rows(source, links):
    piece = source[jnp.maximum(links, 0)]
    keep = (links >= 0).reshape((-1,) + (1,) * (piece.ndim - 1))
    return jnp.where(keep, piece, jnp.zeros((), piece.dtype))


def pad_all(volume, neighbours, channels):
    tiles_count = volume.shape[0]
    deeper = jnp.pad(volume, ((0, 0), (1, 1), (0, 0), (0, 0)))
    above_row = pick_rows(deeper[:, :, H - 1, :], neighbours[:, 0])
    below_row = pick_rows(deeper[:, :, 0, :], neighbours[:, 1])
    tall_block = jnp.concatenate([above_row[:, :, None], deeper, below_row[:, :, None]], axis=2)
    grid_cells = tall_block.reshape(tiles_count, NDISP + 2, H + 2, W, channels)
    left_col = pick_rows(grid_cells[:, :, :, W - 1, :], neighbours[:, 2])
    right_col = pick_rows(grid_cells[:, :, :, 0, :], neighbours[:, 3])
    return jnp.concatenate([left_col[:, :, :, None], grid_cells, right_col[:, :, :, None]], axis=3)


def conv_all(padded, kernel):
    def single_tile(tile_block):
        output = lax.conv_general_dilated(tile_block[None], kernel, (1, 1, 1), "VALID",
                                          dimension_numbers=("NDHWC", "DHWIO", "NDHWC"),
                                          preferred_element_type=jnp.float32)
        return output[0]
    return lax.map(single_tile, padded)


def correlate(tile_features, tile_lines, tile_offsets):
    def cut_band(line_row, begin_at):
        return lax.dynamic_slice_in_dim(line_row, (begin_at * C).astype(jnp.int32), (W + NDISP) * C)
    line_bands = jax.vmap(cut_band)(tile_lines, tile_offsets).reshape(NPV, H, (W + NDISP) * C)
    features = tile_features.astype(jnp.float32)

    def one_shift(shift_step):
        window = lax.dynamic_slice_in_dim(line_bands, (shift_step * C).astype(jnp.int32), W * C, axis=2)
        product = jnp.sum(window.astype(jnp.float32) * features[None], axis=0)
        return product.reshape(H, W * G, C // G).sum(axis=2)
    return lax.map(one_shift, jnp.arange(NDISP, dtype=jnp.int32))


def reference(ref_features, partner_lines, line_owner, line_index, line_offset, neighbours,
              conv1_weight, conv1_bias, conv2_weight, conv2_bias):
    view_of = (jnp.arange(NREQ, dtype=jnp.int32) // H).astype(jnp.int32)
    lines = partner_lines[line_owner[:, :, 0], view_of[None, :], line_index]

    def tile_cost(packed):
        return correlate(packed[0], packed[1], packed[2])
    summed = lax.map(tile_cost, (ref_features, lines, line_offset))
    cost_volume = (summed * (1.0 / (NPV * (C // G)))).astype(jnp.bfloat16)
    first = conv_all(pad_all(cost_volume, neighbours, G), conv1_weight)
    hidden = jax.nn.relu(first + conv1_bias).astype(jnp.bfloat16)
    hidden = hidden.reshape(TILES, NDISP, H, W * CH)
    second = conv_all(pad_all(hidden, neighbours, CH), conv2_weight) + conv2_bias
    return second.reshape(TILES, NDISP, H, W * CH)
```

```python
import jax
import jax.numpy as jnp
import numpy as np
from jax import lax
from jax.experimental import pallas as pl
from jax.experimental.pallas import tpu as pltpu
from jax.sharding import Mesh, PartitionSpec as P

C = 32
G = 8
CH = 32
NDISP = 64
W = 128
NPV = 4
H = 8
LINE = 64
PIECE = 560
SLOTS = 55
PART = SLOTS * 16
BLOCKS = 18
ROWS = BLOCKS * 16
DL = 16
ZB, XB, CB = 8, 4, 2

bf16 = jnp.bfloat16
f32 = jnp.float32


def group_sum_matrix():
    table = np.zeros((256, 256), np.float32)
    for j in range(8):
        for ch in range(C):
            row, g = j * C + ch, ch // 4
            for b in range(3):
                table[row, b * 64 + j * G + g] = 1.0 / 16
                if j == 7:
                    table[row, 192 + b * 16 + g] = 1.0 / 16
                if j == 0:
                    table[row, 192 + b * 16 + 8 + g] = 1.0 / 16
    return np.concatenate([table, table], axis=0)


def taps(cols_in, cols_out):
    picks = np.zeros((len(cols_in), len(cols_out), 3), np.float32)
    for p, j in enumerate(cols_in):
        for q, n in enumerate(cols_out):
            if 0 <= j - n + 1 < 3:
                picks[p, q, j - n + 1] = 1.0
    return picks


def spread_first(kernel):
    out_cols = list(range(8)) + [7, 0] * 3 + [50, 50]
    center = jnp.einsum("jne,abego->abjgno", taps(range(8), out_cols), kernel.astype(f32))
    edges = jnp.einsum("jne,abego->abjgno", taps([-1, 8], out_cols), kernel.astype(f32))
    width = len(out_cols) * CH
    center = center.reshape(3, 192, width)
    edges = edges.reshape(3, 48, width)
    return jnp.concatenate([center, edges, jnp.zeros((3, 16, width), f32)], axis=1).astype(bf16)


def spread_second(kernel):
    center = jnp.einsum("jne,abeko->abjkno", taps(range(8), range(8)), kernel.astype(f32))
    edges = jnp.einsum("jne,abeko->abjkno", taps([-1, 8], range(8)), kernel.astype(f32))
    center = center.reshape(3, 768, 256)
    edges = edges.reshape(3, 192, 256)
    return jnp.concatenate([center, edges, jnp.zeros((3, 64, 256), f32)], axis=1).astype(bf16)


def select_body(tabs, links, where_am_i, pieces, out, stage, padded, shifted):
    tau = where_am_i[0]
    core = where_am_i[1]
    view = where_am_i[2]

    def look(tile, side):
        return jnp.where(tile >= 0, links[jnp.maximum(tile, 0) * 4 + side], -1)

    up, down, left, right = [links[tau * 4 + side] for side in range(4)]
    tiles = [
        [up, look(left, 0), look(right, 0)],
        [tau, left, right],
        [down, look(left, 1), look(right, 1)],
    ]
    stage[...] = jnp.zeros(stage.shape, f32)
    padded[...] = jnp.zeros(padded.shape, f32)
    lane = lax.broadcasted_iota(jnp.int32, (56, 128), 1)

    def put_line(hh, band, column):
        source = tiles[band][column]
        row = hh - 2 if band == 1 else (6 + hh if band == 0 else hh - 10)
        entry = tabs[jnp.maximum(source, 0) * 8 + row]
        owner = entry >> 10
        index = (entry >> 7) & 7
        start = (entry & 127) + 2

        @pl.when((source >= 0) & ((owner & 1) == core))
        def _():
            base = pl.multiple_of((owner >> 1) * PIECE + index * LINE, 16)
            padded[8 : 8 + LINE, :] = pieces[pl.ds(base, LINE), :].astype(f32)
            first = (start >> 2) + 7
            turn = (start & 3) * 32
            lower = padded[pl.ds(first, 56), :]
            upper = padded[pl.ds(first + 1, 56), :]
            shifted[...] = pltpu.roll(
                jnp.where(lane >= turn, lower, upper), (128 - turn) & 127, 1
            )
            for dest in range(4):
                if column == 0:
                    stage[pl.ds(dest * PART + hh, 37, 16), :] = shifted[4 * dest : 4 * dest + 37, :]
                elif column == 1:
                    stage[pl.ds(dest * PART + 37 * 16 + hh, 7, 16), :] = shifted[
                        4 * dest + 30 : 4 * dest + 37, :
                    ]
                else:
                    stage[pl.ds(dest * PART + 44 * 16 + hh, 7, 16), :] = shifted[
                        4 * dest : 4 * dest + 7, :
                    ]

    for hh in range(12):
        for column in range(3):
            put_line(hh, 0 if hh < 2 else (1 if hh < 10 else 2), column)

    halo_center = jnp.where(view < 2, up, down)
    halo_left = jnp.where(view < 2, tiles[0][1], tiles[2][1])
    halo_right = jnp.where(view < 2, tiles[0][2], tiles[2][2])
    halo_row = jnp.where(view < 2, view, view + 8)

    def mine(tile):
        return (tile >= 0) & ((tile & 1) == core)

    def base_of(tile, extra):
        return pl.multiple_of((jnp.maximum(tile, 0) >> 1) * PIECE + extra, 16)

    @pl.when(mine(halo_center))
    def _():
        cells = pieces[pl.ds(base_of(halo_center, 512), 32), :].astype(f32)
        for dest in range(4):
            stage[pl.ds(dest * PART + 12 + view, 32, 16), :] = cells

    def put_pair(cells, slot, row):
        for dest in range(4):
            for k in range(2):
                stage[pl.ds(dest * PART + (slot + k) * 16 + row, 1), :] = cells[k : k + 1]

    @pl.when(mine(halo_left))
    def _():
        cells = pieces[pl.ds(base_of(halo_left, 528), 16), :].astype(f32)
        put_pair(cells[14:16], 51, halo_row)

    @pl.when(mine(halo_right))
    def _():
        cells = pieces[pl.ds(base_of(halo_right, 512), 16), :].astype(f32)
        put_pair(cells[0:2], 53, halo_row)

    @pl.when(mine(left))
    def _():
        cells = pieces[pl.ds(base_of(left, 544), 16), :].astype(f32)
        for k in range(2):
            put_pair(cells[4 * k + 2 : 4 * k + 4], 51, 2 + 2 * view + k)

    @pl.when(mine(right))
    def _():
        cells = pieces[pl.ds(base_of(right, 544), 16), :].astype(f32)
        for k in range(2):
            put_pair(cells[4 * k : 4 * k + 2], 53, 2 + 2 * view + k)

    out[...] = stage[...].astype(bf16)


def select_pieces(tabs, links, where_am_i, pieces):
    return pl.pallas_call(
        select_body,
        out_shape=jax.ShapeDtypeStruct((4 * PART, 128), bf16),
        grid_spec=pltpu.PrefetchScalarGridSpec(
            num_scalar_prefetch=3,
            grid=(1,),
            in_specs=[pl.BlockSpec(pieces.shape, lambda i, *_: (0, 0))],
            out_specs=pl.BlockSpec((4 * PART, 128), lambda i, *_: (0, 0)),
            scratch_shapes=[
                pltpu.VMEM((4 * PART, 128), f32),
                pltpu.VMEM((88, 128), f32),
                pltpu.VMEM((56, 128), f32),
            ],
        ),
        name="select_pieces",
    )(tabs, links, where_am_i, pieces)


def slot_of(block, half):
    if block == 0:
        return 37 + half
    if block == BLOCKS - 1:
        return 44 + half
    return 2 * (block - 1) + half


def volume_body(
    facts, bands, ref, summing, first, first_bias, second, second_bias, out,
    turned, refx, factors, sums, padded, hidden, keep, wide,
):
    view = facts[0]
    lane16 = lax.broadcasted_iota(jnp.int32, (16, 128), 1)
    sub8 = lax.broadcasted_iota(jnp.int32, (8, 128), 0)

    def total(slot):
        cells = bands[slot * 16 : slot * 16 + 16, :].astype(f32)
        for u in range(1, 4):
            at = u * PART + slot * 16
            cells = cells + bands[at : at + 16, :].astype(f32)
        return cells

    lanes = [lane16 >= 32 * m for m in range(4)]
    current = total(0)
    for slot in range(51):
        following = total(slot + 1)
        turned[slot] = current
        for m in range(1, 4):
            turned[m * 51 + slot] = pltpu.roll(
                jnp.where(lanes[m], current, following), 128 - 32 * m, 1
            )
        if slot < 32:
            block, half = 1 + slot // 2, slot % 2
            halo = pltpu.roll(current[8:16], 4, 0)
            own = pltpu.roll(ref[:, slot * 128 : slot * 128 + 128].astype(f32), 2, 0)
            refx[block * 2 + half, 0:8] = jnp.where(sub8 < 2, halo, own)
            refx[block * 2 + half, 8:16] = jnp.where(sub8 < 2, own, halo)
        current = following
    for half in range(2):
        refx[half] = total(51 + half)
        refx[2 * (BLOCKS - 1) + half] = total(53 + half)

    row = lax.broadcasted_iota(jnp.int32, (ROWS, 128), 0)
    high, block = row & 15, row >> 4
    inside = (high >= jnp.where(facts[1] >= 0, 0, 1)) & (high <= jnp.where(facts[2] >= 0, 9, 8))
    inside &= (block >= jnp.where(facts[3] >= 0, 0, 1))
    inside &= (block <= jnp.where(facts[4] >= 0, BLOCKS - 1, BLOCKS - 2))
    keep[...] = jnp.where(inside, 1.0, 0.0)
    sums[ROWS:, :] = jnp.zeros((sums.shape[0] - ROWS, 256), f32)
    hidden[ROWS:, :] = jnp.zeros((hidden.shape[0] - ROWS, 512), f32)

    def cost_step(q, carry):
        for m in range(4):
            dd = 4 * q + m
            for block in range(BLOCKS):
                for half in range(2):
                    product = refx[2 * block + half] * turned[m * 51 + slot_of(block, half) + q]
                    top = product.astype(bf16)
                    rest = (product - top.astype(f32)).astype(bf16)
                    at = block * 16
                    factors[at : at + 16, half * 128 : half * 128 + 128] = top
                    factors[at : at + 16, 256 + half * 128 : 384 + half * 128] = rest
            cells = jnp.dot(factors[...], summing[...], preferred_element_type=f32)
            depth = 16 * view + dd - 2
            sums[0:ROWS, :] = jnp.where((depth >= 0) & (depth < NDISP), cells, 0.0)
            for block in range(BLOCKS):
                at = block * 16
                lo = max(block - 1, 0) * 16
                hi = min(block + 1, BLOCKS - 1) * 16
                left = jnp.where(lane16 < 64, sums[at : at + 16, 0:128], sums[at + 1 : at + 17, 0:128])
                half = sums[at + 2 : at + 18, 128:256]
                for b in range(3):
                    half = jnp.where(lane16 >= 64 + 16 * b, sums[lo + b : lo + b + 16, 128:256], half)
                    half = jnp.where(lane16 >= 72 + 16 * b, sums[hi + b : hi + b + 16, 128:256], half)
                line = pl.multiple_of(dd * ROWS + at, 16)
                padded[pl.ds(line, 16), 0:128] = left.astype(bf16)
                padded[pl.ds(line, 16), 128:256] = half.astype(bf16)
        return carry

    lax.fori_loop(0, 5, cost_step, 0)

    lane8 = lax.broadcasted_iota(jnp.int32, (8, 128), 1)

    def hidden_step(step, carry):
        cells = jnp.broadcast_to(first_bias[...], (ROWS, 512))
        for a in range(3):
            at = pl.multiple_of((step + a) * ROWS, 16)
            cells = cells + jnp.dot(padded[pl.ds(at, ROWS), :], first[a], preferred_element_type=f32)
        depth = 16 * view + step - 1
        live = jnp.where((depth >= 0) & (depth < NDISP), keep[...], 0.0) > 0.5
        for part in range(4):
            span = slice(part * 128, part * 128 + 128)
            hidden[0:ROWS, span] = jnp.where(live, jnp.maximum(cells[:, span], 0.0), 0.0)

        def block_cells(block):
            at, lo, hi = block * 16, (block - 1) * 16, (block + 1) * 16
            parts = []
            for b in range(3):
                parts.append(hidden[at + b : at + b + 8, 0:128])
                parts.append(hidden[at + b : at + b + 8, 128:256])
            edge = hidden[hi + 1 : hi + 9, 256:384]
            edge = jnp.where(lane8 < 96, hidden[lo + 1 : lo + 9, 256:384], edge)
            edge = jnp.where(lane8 < 64, hidden[hi : hi + 8, 256:384], edge)
            parts.append(jnp.where(lane8 < 32, hidden[lo : lo + 8, 256:384], edge))
            edge = hidden[hi + 2 : hi + 10, 384:512]
            parts.append(jnp.where(lane8 < 32, hidden[lo + 2 : lo + 10, 384:512], edge))
            return parts

        for pair in range(8):
            one = block_cells(1 + 2 * pair)
            two = block_cells(2 + 2 * pair)
            at = pl.multiple_of(step * 128 + pair * 16, 16)
            for part in range(8):
                wide[pl.ds(at, 16), part * 128 : part * 128 + 128] = jnp.concatenate(
                    [one[part], two[part]], axis=0
                ).astype(bf16)
        return carry

    lax.fori_loop(0, DL + 2, hidden_step, 0)

    def output_step(step, carry):
        cells = jnp.broadcast_to(second_bias[...], (512, 256))
        for a in range(3):
            at = pl.multiple_of((step * 4 + a) * 128, 128)
            cells = cells + jnp.dot(wide[pl.ds(at, 512), :], second[a], preferred_element_type=f32)
        for d in range(4):
            for block in range(16):
                at = d * 128 + block * 8
                out[step * 4 + d, :, block * 256 : block * 256 + 256] = cells[at : at + 8, :]
        return carry

    lax.fori_loop(0, 4, output_step, 0)


def volume(facts, bands, ref, first, first_bias, second, second_bias):
    operands = (bands, ref, jnp.asarray(group_sum_matrix(), bf16), first, first_bias, second, second_bias)

    def whole(x):
        return pl.BlockSpec(x.shape, lambda i, *_: (0,) * x.ndim)

    return pl.pallas_call(
        volume_body,
        out_shape=jax.ShapeDtypeStruct((DL, H, W * CH), f32),
        grid_spec=pltpu.PrefetchScalarGridSpec(
            num_scalar_prefetch=1,
            grid=(1,),
            in_specs=[whole(x) for x in operands],
            out_specs=pl.BlockSpec((DL, H, W * CH), lambda i, *_: (0, 0, 0)),
            scratch_shapes=[
                pltpu.VMEM((4 * 51, 16, 128), f32),
                pltpu.VMEM((2 * BLOCKS, 16, 128), f32),
                pltpu.VMEM((ROWS, 512), bf16),
                pltpu.VMEM((ROWS + 16, 256), f32),
                pltpu.VMEM((20 * ROWS, 256), bf16),
                pltpu.VMEM((ROWS + 16, 512), f32),
                pltpu.VMEM((ROWS, 128), f32),
                pltpu.VMEM((18 * 128, 1024), bf16),
            ],
        ),
        name="volume",
    )(facts, *operands)


def on_device(
    ref_features, partner_lines, line_owner, line_index, line_offset, neighbours,
    conv1_weight, conv1_bias, conv2_weight, conv2_bias,
):
    view = lax.axis_index("views")
    core = lax.axis_index("c")
    tile = (lax.axis_index("z") * XB + lax.axis_index("x")) * CB + core
    ref = ref_features[0]

    lines = lax.dynamic_index_in_dim(partner_lines[0], view, 0, keepdims=False)
    halo_row = lax.dynamic_slice_in_dim(ref, (view + 6) % 8, 1, axis=0)
    sides = lax.dynamic_slice_in_dim(ref, 2 * view, 2, axis=0)
    sides = jnp.concatenate([sides[:, 0:256], sides[:, 3840:4096]], axis=1)
    payload = jnp.concatenate(
        [
            lines.reshape(8 * LINE, 128),
            halo_row.reshape(32, 128),
            sides.reshape(8, 128),
            jnp.zeros((8, 128), bf16),
        ],
        axis=0,
    )
    row = lax.all_gather(payload, "x", axis=0, tiled=True)
    pieces = lax.all_gather(row, "z", axis=0, tiled=True)

    coded = line_owner[0, :, 0] * 1024 + line_index[0] * 128 + line_offset[0]
    coded = lax.dynamic_slice_in_dim(coded, view * 8, 8)
    tabs = lax.all_to_all(
        jnp.broadcast_to(coded[None], (64, 8)), ("z", "x", "c"), split_axis=0, concat_axis=0, tiled=True
    ).reshape(512)
    links = neighbours.reshape(256)

    other = tile + 1 - 2 * core
    theirs = select_pieces(tabs, links, jnp.stack([other, core, view]), pieces)
    swapped = lax.ppermute(theirs, "c", [(0, 1), (1, 0)])
    own = select_pieces(tabs, links, jnp.stack([tile, core, view]), pieces)
    bands = lax.all_to_all(own + swapped, "views", split_axis=0, concat_axis=0, tiled=True)

    facts = jnp.concatenate([view[None], neighbours[tile]])
    first = spread_first(conv1_weight)
    second = spread_second(conv2_weight)
    first_bias = jnp.tile(conv1_bias, 16)[None]
    second_bias = jnp.tile(conv2_bias, 8)[None]
    return volume(facts, bands, ref, first, first_bias, second, second_bias)[None]


def solution(mesh):
    fine = Mesh(mesh.devices.reshape(ZB, XB, CB, NPV), ("z", "x", "c", "views"))
    tiles = ("z", "x", "c")
    return jax.shard_map(
        on_device,
        mesh=fine,
        in_specs=(
            P(tiles, None, None),
            P(tiles, None, None, None),
            P(tiles, None, None),
            P(tiles, None),
            P(tiles, None),
            P(),
            P(),
            P(),
            P(),
            P(),
        ),
        out_specs=P(tiles, "views", None, None),
        check_vma=False,
    )
```

```python
import jax
import jax.numpy as jnp
import numpy as np
from jax import lax
from jax.experimental import pallas as pl
from jax.experimental.pallas import tpu as pltpu
from jax.sharding import Mesh, PartitionSpec as P

C = 32
G = 8
CH = 32
NDISP = 64
W = 128
NPV = 4
H = 8
LINE = 64
PIECE = 560
SLOTS = 55
PART = SLOTS * 16
BLOCKS = 18
ROWS = BLOCKS * 16
DL = 16
ZB, XB, CB = 8, 4, 2

bf16 = jnp.bfloat16
f32 = jnp.float32


def group_sum_matrix():
    table = np.zeros((256, 256), np.float32)
    for j in range(8):
        for ch in range(C):
            row, g = j * C + ch, ch // 4
            for b in range(3):
                table[row, b * 64 + j * G + g] = 1.0 / 16
                if j == 7:
                    table[row, 192 + b * 16 + g] = 1.0 / 16
                if j == 0:
                    table[row, 192 + b * 16 + 8 + g] = 1.0 / 16
    return np.concatenate([table, table], axis=0)


def taps(cols_in, cols_out):
    picks = np.zeros((len(cols_in), len(cols_out), 3), np.float32)
    for p, j in enumerate(cols_in):
        for q, n in enumerate(cols_out):
            if 0 <= j - n + 1 < 3:
                picks[p, q, j - n + 1] = 1.0
    return picks


def spread_first(kernel):
    out_cols = list(range(8)) + [7, 0] * 3 + [50, 50]
    center = jnp.einsum("jne,abego->abjgno", taps(range(8), out_cols), kernel.astype(f32))
    edges = jnp.einsum("jne,abego->abjgno", taps([-1, 8], out_cols), kernel.astype(f32))
    width = len(out_cols) * CH
    center = center.reshape(3, 192, width)
    edges = edges.reshape(3, 48, width)
    return jnp.concatenate([center, edges, jnp.zeros((3, 16, width), f32)], axis=1).astype(bf16)


def spread_second(kernel):
    center = jnp.einsum("jne,abeko->abjkno", taps(range(8), range(8)), kernel.astype(f32))
    edges = jnp.einsum("jne,abeko->abjkno", taps([-1, 8], range(8)), kernel.astype(f32))
    center = center.reshape(3, 768, 256)
    edges = edges.reshape(3, 192, 256)
    return jnp.concatenate([center, edges, jnp.zeros((3, 64, 256), f32)], axis=1).astype(bf16)


def select_body(tabs, links, where_am_i, pieces, out, stage, padded, shifted):
    tau = where_am_i[0]
    core = where_am_i[1]
    view = where_am_i[2]

    def look(tile, side):
        return jnp.where(tile >= 0, links[jnp.maximum(tile, 0) * 4 + side], -1)

    up, down, left, right = [links[tau * 4 + side] for side in range(4)]
    tiles = [
        [up, look(left, 0), look(right, 0)],
        [tau, left, right],
        [down, look(left, 1), look(right, 1)],
    ]
    stage[...] = jnp.zeros(stage.shape, f32)
    padded[...] = jnp.zeros(padded.shape, f32)
    lane = lax.broadcasted_iota(jnp.int32, (56, 128), 1)

    def put_line(hh, band, column):
        source = tiles[band][column]
        row = hh - 2 if band == 1 else (6 + hh if band == 0 else hh - 10)
        entry = tabs[jnp.maximum(source, 0) * 8 + row]
        owner = entry >> 10
        index = (entry >> 7) & 7
        start = (entry & 127) + 2

        @pl.when((source >= 0) & ((owner & 1) == core))
        def _():
            base = pl.multiple_of((owner >> 1) * PIECE + index * LINE, 16)
            padded[8 : 8 + LINE, :] = pieces[pl.ds(base, LINE), :].astype(f32)
            first = (start >> 2) + 7
            turn = (start & 3) * 32
            lower = padded[pl.ds(first, 56), :]
            upper = padded[pl.ds(first + 1, 56), :]
            shifted[...] = pltpu.roll(
                jnp.where(lane >= turn, lower, upper), (128 - turn) & 127, 1
            )
            for dest in range(4):
                if column == 0:
                    stage[pl.ds(dest * PART + hh, 37, 16), :] = shifted[4 * dest : 4 * dest + 37, :]
                elif column == 1:
                    stage[pl.ds(dest * PART + 37 * 16 + hh, 7, 16), :] = shifted[
                        4 * dest + 30 : 4 * dest + 37, :
                    ]
                else:
                    stage[pl.ds(dest * PART + 44 * 16 + hh, 7, 16), :] = shifted[
                        4 * dest : 4 * dest + 7, :
                    ]

    for hh in range(12):
        for column in range(3):
            put_line(hh, 0 if hh < 2 else (1 if hh < 10 else 2), column)

    halo_center = jnp.where(view < 2, up, down)
    halo_left = jnp.where(view < 2, tiles[0][1], tiles[2][1])
    halo_right = jnp.where(view < 2, tiles[0][2], tiles[2][2])
    halo_row = jnp.where(view < 2, view, view + 8)

    def mine(tile):
        return (tile >= 0) & ((tile & 1) == core)

    def base_of(tile, extra):
        return pl.multiple_of((jnp.maximum(tile, 0) >> 1) * PIECE + extra, 16)

    @pl.when(mine(halo_center))
    def _():
        cells = pieces[pl.ds(base_of(halo_center, 512), 32), :].astype(f32)
        for dest in range(4):
            stage[pl.ds(dest * PART + 12 + view, 32, 16), :] = cells

    def put_pair(cells, slot, row):
        for dest in range(4):
            for k in range(2):
                stage[pl.ds(dest * PART + (slot + k) * 16 + row, 1), :] = cells[k : k + 1]

    @pl.when(mine(halo_left))
    def _():
        cells = pieces[pl.ds(base_of(halo_left, 528), 16), :].astype(f32)
        put_pair(cells[14:16], 51, halo_row)

    @pl.when(mine(halo_right))
    def _():
        cells = pieces[pl.ds(base_of(halo_right, 512), 16), :].astype(f32)
        put_pair(cells[0:2], 53, halo_row)

    @pl.when(mine(left))
    def _():
        cells = pieces[pl.ds(base_of(left, 544), 16), :].astype(f32)
        for k in range(2):
            put_pair(cells[4 * k + 2 : 4 * k + 4], 51, 2 + 2 * view + k)

    @pl.when(mine(right))
    def _():
        cells = pieces[pl.ds(base_of(right, 544), 16), :].astype(f32)
        for k in range(2):
            put_pair(cells[4 * k : 4 * k + 2], 53, 2 + 2 * view + k)

    out[...] = stage[...].astype(bf16)


def select_pieces(tabs, links, where_am_i, pieces):
    return pl.pallas_call(
        select_body,
        out_shape=jax.ShapeDtypeStruct((4 * PART, 128), bf16),
        grid_spec=pltpu.PrefetchScalarGridSpec(
            num_scalar_prefetch=3,
            grid=(1,),
            in_specs=[pl.BlockSpec(pieces.shape, lambda i, *_: (0, 0))],
            out_specs=pl.BlockSpec((4 * PART, 128), lambda i, *_: (0, 0)),
            scratch_shapes=[
                pltpu.VMEM((4 * PART, 128), f32),
                pltpu.VMEM((88, 128), f32),
                pltpu.VMEM((56, 128), f32),
            ],
        ),
        name="select_pieces",
    )(tabs, links, where_am_i, pieces)


def slot_of(block, half):
    if block == 0:
        return 37 + half
    if block == BLOCKS - 1:
        return 44 + half
    return 2 * (block - 1) + half


def volume_body(
    facts, bands, ref, summing, first, first_bias, second, second_bias, out,
    turned, refx, factors, sums, padded, hidden, keep, wide,
):
    view = facts[0]
    lane16 = lax.broadcasted_iota(jnp.int32, (16, 128), 1)
    sub8 = lax.broadcasted_iota(jnp.int32, (8, 128), 0)

    def total(slot):
        cells = bands[slot * 16 : slot * 16 + 16, :].astype(f32)
        for u in range(1, 4):
            at = u * PART + slot * 16
            cells = cells + bands[at : at + 16, :].astype(f32)
        return cells

    lanes = [lane16 >= 32 * m for m in range(4)]
    current = total(0)
    for slot in range(51):
        following = total(slot + 1)
        turned[slot] = current
        for m in range(1, 4):
            turned[m * 51 + slot] = pltpu.roll(
                jnp.where(lanes[m], current, following), 128 - 32 * m, 1
            )
        if slot < 32:
            block, half = 1 + slot // 2, slot % 2
            halo = pltpu.roll(current[8:16], 4, 0)
            own = pltpu.roll(ref[:, slot * 128 : slot * 128 + 128].astype(f32), 2, 0)
            refx[block * 2 + half, 0:8] = jnp.where(sub8 < 2, halo, own)
            refx[block * 2 + half, 8:16] = jnp.where(sub8 < 2, own, halo)
        current = following
    for half in range(2):
        refx[half] = total(51 + half)
        refx[2 * (BLOCKS - 1) + half] = total(53 + half)

    row = lax.broadcasted_iota(jnp.int32, (ROWS, 128), 0)
    high, block = row & 15, row >> 4
    inside = (high >= jnp.where(facts[1] >= 0, 0, 1)) & (high <= jnp.where(facts[2] >= 0, 9, 8))
    inside &= (block >= jnp.where(facts[3] >= 0, 0, 1))
    inside &= (block <= jnp.where(facts[4] >= 0, BLOCKS - 1, BLOCKS - 2))
    keep[...] = jnp.where(inside, 1.0, 0.0)
    sums[ROWS:, :] = jnp.zeros((sums.shape[0] - ROWS, 256), f32)
    hidden[ROWS:, :] = jnp.zeros((hidden.shape[0] - ROWS, 512), f32)

    def cost_step(q, carry):
        for m in range(4):
            dd = 4 * q + m
            for block in range(BLOCKS):
                for half in range(2):
                    product = refx[2 * block + half] * turned[m * 51 + slot_of(block, half) + q]
                    top = product.astype(bf16)
                    rest = (product - top.astype(f32)).astype(bf16)
                    at = block * 16
                    factors[at : at + 16, half * 128 : half * 128 + 128] = top
                    factors[at : at + 16, 256 + half * 128 : 384 + half * 128] = rest
            cells = jnp.dot(factors[...], summing[...], preferred_element_type=f32)
            depth = 16 * view + dd - 2
            sums[0:ROWS, :] = jnp.where((depth >= 0) & (depth < NDISP), cells, 0.0)
            for block in range(BLOCKS):
                at = block * 16
                lo = max(block - 1, 0) * 16
                hi = min(block + 1, BLOCKS - 1) * 16
                left = jnp.where(lane16 < 64, sums[at : at + 16, 0:128], sums[at + 1 : at + 17, 0:128])
                half = sums[at + 2 : at + 18, 128:256]
                for b in range(3):
                    half = jnp.where(lane16 >= 64 + 16 * b, sums[lo + b : lo + b + 16, 128:256], half)
                    half = jnp.where(lane16 >= 72 + 16 * b, sums[hi + b : hi + b + 16, 128:256], half)
                line = pl.multiple_of(dd * ROWS + at, 16)
                padded[pl.ds(line, 16), 0:128] = left.astype(bf16)
                padded[pl.ds(line, 16), 128:256] = half.astype(bf16)
        return carry

    lax.fori_loop(0, 5, cost_step, 0)

    lane8 = lax.broadcasted_iota(jnp.int32, (8, 128), 1)

    def hidden_step(step, carry):
        cells = jnp.broadcast_to(first_bias[...], (ROWS, 512))
        for a in range(3):
            at = pl.multiple_of((step + a) * ROWS, 16)
            cells = cells + jnp.dot(padded[pl.ds(at, ROWS), :], first[a], preferred_element_type=f32)
        depth = 16 * view + step - 1
        live = jnp.where((depth >= 0) & (depth < NDISP), keep[...], 0.0) > 0.5
        for part in range(4):
            span = slice(part * 128, part * 128 + 128)
            hidden[0:ROWS, span] = jnp.where(live, jnp.maximum(cells[:, span], 0.0), 0.0)

        def block_cells(block):
            at, lo, hi = block * 16, (block - 1) * 16, (block + 1) * 16
            parts = []
            for b in range(3):
                parts.append(hidden[at + b : at + b + 8, 0:128])
                parts.append(hidden[at + b : at + b + 8, 128:256])
            edge = hidden[hi + 1 : hi + 9, 256:384]
            edge = jnp.where(lane8 < 96, hidden[lo + 1 : lo + 9, 256:384], edge)
            edge = jnp.where(lane8 < 64, hidden[hi : hi + 8, 256:384], edge)
            parts.append(jnp.where(lane8 < 32, hidden[lo : lo + 8, 256:384], edge))
            edge = hidden[hi + 2 : hi + 10, 384:512]
            parts.append(jnp.where(lane8 < 32, hidden[lo + 2 : lo + 10, 384:512], edge))
            return parts

        for pair in range(8):
            one = block_cells(1 + 2 * pair)
            two = block_cells(2 + 2 * pair)
            at = pl.multiple_of(step * 128 + pair * 16, 16)
            for part in range(8):
                wide[pl.ds(at, 16), part * 128 : part * 128 + 128] = jnp.concatenate(
                    [one[part], two[part]], axis=0
                ).astype(bf16)
        return carry

    lax.fori_loop(0, DL + 2, hidden_step, 0)

    def output_step(step, carry):
        cells = jnp.broadcast_to(second_bias[...], (512, 256))
        for a in range(3):
            at = pl.multiple_of((step * 4 + a) * 128, 128)
            cells = cells + jnp.dot(wide[pl.ds(at, 512), :], second[a], preferred_element_type=f32)
        for d in range(4):
            for block in range(16):
                at = d * 128 + block * 8
                out[step * 4 + d, :, block * 256 : block * 256 + 256] = cells[at : at + 8, :]
        return carry

    lax.fori_loop(0, 4, output_step, 0)


def volume(facts, bands, ref, first, first_bias, second, second_bias):
    operands = (bands, ref, jnp.asarray(group_sum_matrix(), bf16), first, first_bias, second, second_bias)

    def whole(x):
        return pl.BlockSpec(x.shape, lambda i, *_: (0,) * x.ndim)

    return pl.pallas_call(
        volume_body,
        out_shape=jax.ShapeDtypeStruct((DL, H, W * CH), f32),
        grid_spec=pltpu.PrefetchScalarGridSpec(
            num_scalar_prefetch=1,
            grid=(1,),
            in_specs=[whole(x) for x in operands],
            out_specs=pl.BlockSpec((DL, H, W * CH), lambda i, *_: (0, 0, 0)),
            scratch_shapes=[
                pltpu.VMEM((4 * 51, 16, 128), f32),
                pltpu.VMEM((2 * BLOCKS, 16, 128), f32),
                pltpu.VMEM((ROWS, 512), bf16),
                pltpu.VMEM((ROWS + 16, 256), f32),
                pltpu.VMEM((20 * ROWS, 256), bf16),
                pltpu.VMEM((ROWS + 16, 512), f32),
                pltpu.VMEM((ROWS, 128), f32),
                pltpu.VMEM((18 * 128, 1024), bf16),
            ],
        ),
        name="volume",
    )(facts, *operands)


def on_device(
    ref_features, partner_lines, line_owner, line_index, line_offset, neighbours,
    conv1_weight, conv1_bias, conv2_weight, conv2_bias,
):
    view = lax.axis_index("views")
    core = lax.axis_index("c")
    tile = (lax.axis_index("z") * XB + lax.axis_index("x")) * CB + core
    ref = ref_features[0]

    lines = lax.dynamic_index_in_dim(partner_lines[0], view, 0, keepdims=False)
    halo_row = lax.dynamic_slice_in_dim(ref, (view + 6) % 8, 1, axis=0)
    sides = lax.dynamic_slice_in_dim(ref, 2 * view, 2, axis=0)
    sides = jnp.concatenate([sides[:, 0:256], sides[:, 3840:4096]], axis=1)
    payload = jnp.concatenate(
        [
            lines.reshape(8 * LINE, 128),
            halo_row.reshape(32, 128),
            sides.reshape(8, 128),
            jnp.zeros((8, 128), bf16),
        ],
        axis=0,
    )
    row = lax.all_gather(payload, "x", axis=0, tiled=True)
    pieces = lax.all_gather(row, "z", axis=0, tiled=True)

    coded = line_owner[0, :, 0] * 1024 + line_index[0] * 128 + line_offset[0]
    coded = lax.dynamic_slice_in_dim(coded, view * 8, 8)
    tabs = lax.all_to_all(
        jnp.broadcast_to(coded[None], (64, 8)), ("z", "x", "c"), split_axis=0, concat_axis=0, tiled=True
    ).reshape(512)
    links = neighbours.reshape(256)

    first = spread_first(conv1_weight)
    second = spread_second(conv2_weight)
    first_bias = jnp.tile(conv1_bias, 16)[None]
    second_bias = jnp.tile(conv2_bias, 8)[None]
    facts = jnp.concatenate([view[None], neighbours[tile]])
    other = tile + 1 - 2 * core
    tabs, links, first, second, first_bias, second_bias, facts = lax.optimization_barrier(
        (tabs, links, first, second, first_bias, second_bias, facts)
    )
    theirs = select_pieces(tabs, links, jnp.stack([other, core, view]), pieces)
    swapped = lax.ppermute(theirs, "c", [(0, 1), (1, 0)])
    own = select_pieces(tabs, links, jnp.stack([tile, core, view]), pieces)
    bands = lax.all_to_all(own + swapped, "views", split_axis=0, concat_axis=0, tiled=True)

    return volume(facts, bands, ref, first, first_bias, second, second_bias)[None]


def solution(mesh):
    fine = Mesh(mesh.devices.reshape(ZB, XB, CB, NPV), ("z", "x", "c", "views"))
    tiles = ("z", "x", "c")
    return jax.shard_map(
        on_device,
        mesh=fine,
        in_specs=(
            P(tiles, None, None),
            P(tiles, None, None, None),
            P(tiles, None, None),
            P(tiles, None),
            P(tiles, None),
            P(),
            P(),
            P(),
            P(),
            P(),
        ),
        out_specs=P(tiles, "views", None, None),
        check_vma=False,
    )
```

```python
import jax
import jax.numpy as jnp
import numpy as np
from jax import lax
from jax.experimental import pallas as pl
from jax.experimental.pallas import tpu as pltpu
from jax.sharding import Mesh, PartitionSpec as P

C = 32
G = 8
CH = 32
NDISP = 64
W = 128
NPV = 4
H = 8
LINE = 64
PIECE = 560
SLOTS = 55
PART = SLOTS * 16
BLOCKS = 18
ROWS = BLOCKS * 16
DL = 16
ZB, XB, CB = 8, 4, 2

bf16 = jnp.bfloat16
f32 = jnp.float32


def group_sum_matrix():
    table = np.zeros((256, 256), np.float32)
    for j in range(8):
        for ch in range(C):
            row, g = j * C + ch, ch // 4
            for b in range(3):
                table[row, b * 64 + j * G + g] = 1.0 / 16
                if j == 7:
                    table[row, 192 + b * 16 + g] = 1.0 / 16
                if j == 0:
                    table[row, 192 + b * 16 + 8 + g] = 1.0 / 16
    return np.concatenate([table, table], axis=0)


def spread_body(k1, k2, first, second):
    def repeat(cells, count):
        row = lax.broadcasted_iota(jnp.int32, (CH, count * CH), 0)
        lane = lax.broadcasted_iota(jnp.int32, (CH, count * CH), 1)
        copies = jnp.where((lane & 31) == row, 1.0, 0.0).astype(bf16)
        return jnp.dot(cells, copies, preferred_element_type=f32)

    wide1 = repeat(k1[...], 16)
    wide2 = repeat(k2[...], 8)
    lane1 = lax.broadcasted_iota(jnp.int32, (8, 512), 1) >> 5
    lane2 = lax.broadcasted_iota(jnp.int32, (CH, 256), 1) >> 5
    col1 = jnp.where(lane1 < 8, lane1, jnp.where(lane1 < 14, jnp.where((lane1 & 1) == 0, 7, 0), 50))

    def line(cells, depth, a, b, j, col):
        result = jnp.zeros(col.shape, f32)
        for e in range(3):
            at = ((a * 3 + b) * 3 + e) * depth
            result = jnp.where(col == j + 1 - e, cells[at : at + depth], result)
        return result

    for a in range(3):
        for b in range(3):
            for j in range(0, 8, 2):
                pair = [line(wide1, G, a, b, j + i, col1) for i in range(2)]
                first[a, b * 64 + j * 8 : b * 64 + j * 8 + 16, :] = jnp.concatenate(pair, 0).astype(bf16)
            pair = [line(wide1, G, a, b, j, col1) for j in (-1, 8)]
            first[a, 192 + b * 16 : 208 + b * 16, :] = jnp.concatenate(pair, 0).astype(bf16)
            for j in range(8):
                at = b * 256 + j * 32
                second[a, at : at + 32, :] = line(wide2, CH, a, b, j, lane2).astype(bf16)
            for side, j in enumerate((-1, 8)):
                at = 768 + b * 64 + side * 32
                second[a, at : at + 32, :] = line(wide2, CH, a, b, j, lane2).astype(bf16)
        first[a, 240:256, :] = jnp.zeros((16, 512), bf16)
        second[a, 960:1024, :] = jnp.zeros((64, 256), bf16)


def spread_weights(k1, k2):
    return pl.pallas_call(
        spread_body,
        out_shape=(
            jax.ShapeDtypeStruct((3, 256, 512), bf16),
            jax.ShapeDtypeStruct((3, 1024, 256), bf16),
        ),
        name="spread_weights",
    )(k1.reshape(27 * G, CH), k2.reshape(27 * CH, CH))


def select_body(links, where_am_i, *refs):
    chunks = refs[:16]
    out, pieces, stage, padded, shifted, rows, tabs, arrived, listed = refs[16:]
    tau = where_am_i[0]
    core = where_am_i[1]
    view = where_am_i[2]
    here = where_am_i[3]

    copies = []
    for spot, chunk in enumerate(chunks):
        at = spot * 2 * PIECE
        copies.append(
            pltpu.make_async_copy(chunk, pieces.at[at : at + 2 * PIECE], arrived.at[spot])
        )
        copies[-1].start()

    def home(owner):
        dz = ((owner >> 3) - (here >> 3)) & 7
        dx = ((owner >> 1) - (here >> 1)) & 3
        turn = jnp.where(dx == 0, 0, jnp.where(dx == 3, 1, dx + 1))
        return dz * 4 + turn

    def look(tile, side):
        return jnp.where(tile >= 0, links[jnp.maximum(tile, 0) * 4 + side], -1)

    up, down, left, right = [links[tau * 4 + side] for side in range(4)]
    tiles = [
        [up, look(left, 0), look(right, 0)],
        [tau, left, right],
        [down, look(left, 1), look(right, 1)],
    ]
    stage[...] = jnp.zeros(stage.shape, f32)
    padded[...] = jnp.zeros(padded.shape, f32)
    lane = lax.broadcasted_iota(jnp.int32, (56, 128), 1)
    for copy in copies:
        copy.wait()
    for spot in range(32):
        cells = pieces[spot * PIECE + 544 : spot * PIECE + 560, :].astype(f32)
        rows[spot : spot + 1, :] = cells[8:9].astype(jnp.int32)
    listing = pltpu.make_async_copy(rows, tabs, listed)
    listing.start()
    listing.wait()

    def put_line(hh, band, column):
        source = tiles[band][column]
        row = hh - 2 if band == 1 else (6 + hh if band == 0 else hh - 10)
        known = jnp.maximum(source, 0)
        spot, column_at = home(known), (known & 1) * 24 + row
        owner = tabs[spot, column_at]
        index = tabs[spot, column_at + 8]
        start = tabs[spot, column_at + 16] + 2

        @pl.when((source >= 0) & ((owner & 1) == core))
        def _():
            base = pl.multiple_of(home(owner) * PIECE + index * LINE, 16)
            padded[8 : 8 + LINE, :] = pieces[pl.ds(base, LINE), :].astype(f32)
            first = (start >> 2) + 7
            turn = (start & 3) * 32
            lower = padded[pl.ds(first, 56), :]
            upper = padded[pl.ds(first + 1, 56), :]
            shifted[...] = pltpu.roll(
                jnp.where(lane >= turn, lower, upper), (128 - turn) & 127, 1
            )
            for dest in range(4):
                begin = ((view + dest) & 3) * 4
                if column == 0:
                    stage[pl.ds(dest * PART + hh, 37, 16), :] = shifted[pl.ds(begin, 37), :]
                elif column == 1:
                    stage[pl.ds(dest * PART + 37 * 16 + hh, 7, 16), :] = shifted[pl.ds(begin + 30, 7), :]
                else:
                    stage[pl.ds(dest * PART + 44 * 16 + hh, 7, 16), :] = shifted[pl.ds(begin, 7), :]

    for hh in range(12):
        for column in range(3):
            put_line(hh, 0 if hh < 2 else (1 if hh < 10 else 2), column)

    halo_center = jnp.where(view < 2, up, down)
    halo_left = jnp.where(view < 2, tiles[0][1], tiles[2][1])
    halo_right = jnp.where(view < 2, tiles[0][2], tiles[2][2])
    halo_row = jnp.where(view < 2, view, view + 8)

    def mine(tile):
        return (tile >= 0) & ((tile & 1) == core)

    def base_of(tile, extra):
        return pl.multiple_of(home(jnp.maximum(tile, 0)) * PIECE + extra, 16)

    @pl.when(mine(halo_center))
    def _():
        cells = pieces[pl.ds(base_of(halo_center, 512), 32), :].astype(f32)
        for dest in range(4):
            stage[pl.ds(dest * PART + 12 + view, 32, 16), :] = cells

    def put_pair(cells, slot, row):
        for dest in range(4):
            for k in range(2):
                stage[pl.ds(dest * PART + (slot + k) * 16 + row, 1), :] = cells[k : k + 1]

    @pl.when(mine(halo_left))
    def _():
        cells = pieces[pl.ds(base_of(halo_left, 528), 16), :].astype(f32)
        put_pair(cells[14:16], 51, halo_row)

    @pl.when(mine(halo_right))
    def _():
        cells = pieces[pl.ds(base_of(halo_right, 512), 16), :].astype(f32)
        put_pair(cells[0:2], 53, halo_row)

    @pl.when(mine(left))
    def _():
        cells = pieces[pl.ds(base_of(left, 544), 16), :].astype(f32)
        for k in range(2):
            put_pair(cells[4 * k + 2 : 4 * k + 4], 51, 2 + 2 * view + k)

    @pl.when(mine(right))
    def _():
        cells = pieces[pl.ds(base_of(right, 544), 16), :].astype(f32)
        for k in range(2):
            put_pair(cells[4 * k : 4 * k + 2], 53, 2 + 2 * view + k)

    out[...] = stage[...].astype(bf16)


def select_pieces(links, where_am_i, chunks):
    return pl.pallas_call(
        select_body,
        out_shape=jax.ShapeDtypeStruct((4 * PART, 128), bf16),
        grid_spec=pltpu.PrefetchScalarGridSpec(
            num_scalar_prefetch=2,
            grid=(1,),
            in_specs=[pl.BlockSpec(memory_space=pl.ANY)] * 16,
            out_specs=pl.BlockSpec((4 * PART, 128), lambda i, *_: (0, 0)),
            scratch_shapes=[
                pltpu.VMEM((32 * PIECE, 128), bf16),
                pltpu.VMEM((4 * PART, 128), f32),
                pltpu.VMEM((88, 128), f32),
                pltpu.VMEM((56, 128), f32),
                pltpu.VMEM((32, 128), jnp.int32),
                pltpu.SMEM((32, 128), jnp.int32),
                pltpu.SemaphoreType.DMA((16,)),
                pltpu.SemaphoreType.DMA,
            ],
        ),
        name="select_pieces",
    )(links, where_am_i, *chunks)


def slot_of(block, half):
    if block == 0:
        return 37 + half
    if block == BLOCKS - 1:
        return 44 + half
    return 2 * (block - 1) + half


def volume_body(
    facts, band0, band1, band2, band3, ref, summing, first, first_bias, second, second_bias, out,
    turned, refx, factors, sums, padded, hidden, keep, wide,
):
    view = facts[0]
    lane16 = lax.broadcasted_iota(jnp.int32, (16, 128), 1)
    sub8 = lax.broadcasted_iota(jnp.int32, (8, 128), 0)

    def total(slot):
        span = slice(slot * 16, slot * 16 + 16)
        return (band0[span, :].astype(f32) + band1[span, :].astype(f32)) + (
            band2[span, :].astype(f32) + band3[span, :].astype(f32)
        )

    lanes = [lane16 >= 32 * m for m in range(4)]
    current = total(0)
    for slot in range(51):
        following = total(slot + 1)
        turned[slot] = current
        for m in range(1, 4):
            turned[m * 51 + slot] = pltpu.roll(
                jnp.where(lanes[m], current, following), 128 - 32 * m, 1
            )
        if slot < 32:
            block, half = 1 + slot // 2, slot % 2
            halo = pltpu.roll(current[8:16], 4, 0)
            own = pltpu.roll(ref[:, slot * 128 : slot * 128 + 128].astype(f32), 2, 0)
            refx[block * 2 + half, 0:8] = jnp.where(sub8 < 2, halo, own)
            refx[block * 2 + half, 8:16] = jnp.where(sub8 < 2, own, halo)
        current = following
    for half in range(2):
        refx[half] = total(51 + half)
        refx[2 * (BLOCKS - 1) + half] = total(53 + half)

    row = lax.broadcasted_iota(jnp.int32, (ROWS, 128), 0)
    high, block = row & 15, row >> 4
    inside = (high >= jnp.where(facts[1] >= 0, 0, 1)) & (high <= jnp.where(facts[2] >= 0, 9, 8))
    inside &= (block >= jnp.where(facts[3] >= 0, 0, 1))
    inside &= (block <= jnp.where(facts[4] >= 0, BLOCKS - 1, BLOCKS - 2))
    keep[...] = jnp.where(inside, 1.0, 0.0)
    sums[ROWS:, :] = jnp.zeros((sums.shape[0] - ROWS, 256), f32)
    hidden[ROWS:, :] = jnp.zeros((hidden.shape[0] - ROWS, 512), f32)

    def cost_step(q, carry):
        for m in range(4):
            dd = 4 * q + m
            for block in range(BLOCKS):
                for half in range(2):
                    product = refx[2 * block + half] * turned[m * 51 + slot_of(block, half) + q]
                    top = product.astype(bf16)
                    rest = (product - top.astype(f32)).astype(bf16)
                    at = block * 16
                    factors[at : at + 16, half * 128 : half * 128 + 128] = top
                    factors[at : at + 16, 256 + half * 128 : 384 + half * 128] = rest
            cells = jnp.dot(factors[...], summing[...], preferred_element_type=f32)
            depth = 16 * view + dd - 2
            sums[0:ROWS, :] = jnp.where((depth >= 0) & (depth < NDISP), cells, 0.0)
            for block in range(BLOCKS):
                at = block * 16
                lo = max(block - 1, 0) * 16
                hi = min(block + 1, BLOCKS - 1) * 16
                left = jnp.where(lane16 < 64, sums[at : at + 16, 0:128], sums[at + 1 : at + 17, 0:128])
                half = sums[at + 2 : at + 18, 128:256]
                for b in range(3):
                    half = jnp.where(lane16 >= 64 + 16 * b, sums[lo + b : lo + b + 16, 128:256], half)
                    half = jnp.where(lane16 >= 72 + 16 * b, sums[hi + b : hi + b + 16, 128:256], half)
                line = pl.multiple_of(dd * ROWS + at, 16)
                padded[pl.ds(line, 16), 0:128] = left.astype(bf16)
                padded[pl.ds(line, 16), 128:256] = half.astype(bf16)
        return carry

    lax.fori_loop(0, 5, cost_step, 0)

    lane8 = lax.broadcasted_iota(jnp.int32, (8, 128), 1)

    def hidden_step(step, carry):
        cells = jnp.broadcast_to(first_bias[...], (ROWS, 512))
        for a in range(3):
            at = pl.multiple_of((step + a) * ROWS, 16)
            cells = cells + jnp.dot(padded[pl.ds(at, ROWS), :], first[a], preferred_element_type=f32)
        depth = 16 * view + step - 1
        live = jnp.where((depth >= 0) & (depth < NDISP), keep[...], 0.0) > 0.5
        for part in range(4):
            span = slice(part * 128, part * 128 + 128)
            hidden[0:ROWS, span] = jnp.where(live, jnp.maximum(cells[:, span], 0.0), 0.0)

        def block_cells(block):
            at, lo, hi = block * 16, (block - 1) * 16, (block + 1) * 16
            parts = []
            for b in range(3):
                parts.append(hidden[at + b : at + b + 8, 0:128])
                parts.append(hidden[at + b : at + b + 8, 128:256])
            edge = hidden[hi + 1 : hi + 9, 256:384]
            edge = jnp.where(lane8 < 96, hidden[lo + 1 : lo + 9, 256:384], edge)
            edge = jnp.where(lane8 < 64, hidden[hi : hi + 8, 256:384], edge)
            parts.append(jnp.where(lane8 < 32, hidden[lo : lo + 8, 256:384], edge))
            edge = hidden[hi + 2 : hi + 10, 384:512]
            parts.append(jnp.where(lane8 < 32, hidden[lo + 2 : lo + 10, 384:512], edge))
            return parts

        for pair in range(8):
            one = block_cells(1 + 2 * pair)
            two = block_cells(2 + 2 * pair)
            at = pl.multiple_of(step * 128 + pair * 16, 16)
            for part in range(8):
                wide[pl.ds(at, 16), part * 128 : part * 128 + 128] = jnp.concatenate(
                    [one[part], two[part]], axis=0
                ).astype(bf16)
        return carry

    lax.fori_loop(0, DL + 2, hidden_step, 0)

    def output_step(step, carry):
        cells = jnp.broadcast_to(second_bias[...], (512, 256))
        for a in range(3):
            at = pl.multiple_of((step * 4 + a) * 128, 128)
            cells = cells + jnp.dot(wide[pl.ds(at, 512), :], second[a], preferred_element_type=f32)
        for d in range(4):
            for block in range(16):
                at = d * 128 + block * 8
                out[step * 4 + d, :, block * 256 : block * 256 + 256] = cells[at : at + 8, :]
        return carry

    lax.fori_loop(0, 4, output_step, 0)


def volume(facts, bands, ref, first, first_bias, second, second_bias):
    operands = (*bands, ref, jnp.asarray(group_sum_matrix(), bf16), first, first_bias, second, second_bias)

    def whole(x):
        return pl.BlockSpec(x.shape, lambda i, *_: (0,) * x.ndim)

    return pl.pallas_call(
        volume_body,
        out_shape=jax.ShapeDtypeStruct((DL, H, W * CH), f32),
        grid_spec=pltpu.PrefetchScalarGridSpec(
            num_scalar_prefetch=1,
            grid=(1,),
            in_specs=[whole(x) for x in operands],
            out_specs=pl.BlockSpec((DL, H, W * CH), lambda i, *_: (0, 0, 0)),
            scratch_shapes=[
                pltpu.VMEM((4 * 51, 16, 128), f32),
                pltpu.VMEM((2 * BLOCKS, 16, 128), f32),
                pltpu.VMEM((ROWS, 512), bf16),
                pltpu.VMEM((ROWS + 16, 256), f32),
                pltpu.VMEM((20 * ROWS, 256), bf16),
                pltpu.VMEM((ROWS + 16, 512), f32),
                pltpu.VMEM((ROWS, 128), f32),
                pltpu.VMEM((18 * 128, 1024), bf16),
            ],
        ),
        name="volume",
    )(facts, *operands)


def on_device(
    ref_features, partner_lines, line_owner, line_index, line_offset, neighbours,
    conv1_weight, conv1_bias, conv2_weight, conv2_bias,
):
    view = lax.axis_index("views")
    core = lax.axis_index("c")
    tile = (lax.axis_index("z") * XB + lax.axis_index("x")) * CB + core
    ref = ref_features[0]

    lines = lax.dynamic_index_in_dim(partner_lines[0], view, 0, keepdims=False)
    halo_row = lax.dynamic_slice_in_dim(ref, (view + 6) % 8, 1, axis=0)
    sides = lax.dynamic_slice_in_dim(ref, 2 * view, 2, axis=0)
    sides = jnp.concatenate([sides[:, 0:256], sides[:, 3840:4096]], axis=1)
    names = jnp.stack([line_owner[0, :, 0], line_index[0], line_offset[0]])
    names = lax.dynamic_slice_in_dim(names, view * 8, 8, axis=1).astype(bf16).reshape(24)
    twin = lax.ppermute(names, "c", [(0, 1), (1, 0)])
    names = jnp.where(core == 0, jnp.concatenate([names, twin]), jnp.concatenate([twin, names]))
    payload = jnp.concatenate(
        [
            lines.reshape(8 * LINE, 128),
            halo_row.reshape(32, 128),
            sides.reshape(8, 128),
            jnp.pad(names[None], ((0, 7), (0, 80))),
        ],
        axis=0,
    )
    def shift(x, axis, by):
        count = lax.axis_size(axis)
        return lax.ppermute(x, axis, [(i, (i + by) % count) for i in range(count)])

    one, two, three = shift(payload, "x", 1), shift(payload, "x", -1), shift(payload, "x", 2)
    chunks = [[None, None] for _ in range(8)]
    chunks[0] = [jnp.concatenate([payload, one]), jnp.concatenate([two, three])]
    for k in range(1, 4):
        for i in range(2):
            chunks[-k % 8][i] = shift(chunks[(1 - k) % 8][i], "z", 1)
            chunks[k][i] = shift(chunks[k - 1][i], "z", -1)
    chunks[4] = [shift(chunks[5][0], "z", 1), shift(chunks[3][1], "z", -1)]
    chunks = [chunk for pair in chunks for chunk in pair]

    links = neighbours.reshape(256)

    first, second = spread_weights(conv1_weight, conv2_weight)
    first_bias = jnp.tile(conv1_bias, 16)[None]
    second_bias = jnp.tile(conv2_bias, 8)[None]
    facts = jnp.concatenate([view[None], neighbours[tile]])
    other = tile + 1 - 2 * core
    asked = jnp.stack([other, core, view, tile])
    wanted = jnp.stack([tile, core, view, tile])
    links, asked, wanted, first, second, first_bias, second_bias, facts = lax.optimization_barrier(
        (links, asked, wanted, first, second, first_bias, second_bias, facts)
    )
    theirs = select_pieces(links, asked, chunks)
    swapped = lax.ppermute(theirs, "c", [(0, 1), (1, 0)])
    own = select_pieces(links, wanted, chunks)

    def part(step):
        span = slice(step * PART, (step + 1) * PART)
        return own[span] + swapped[span]

    bands = [part(0)] + [shift(part(step), "views", step) for step in (1, 2, 3)]
    return volume(facts, bands, ref, first, first_bias, second, second_bias)[None]


def solution(mesh):
    fine = Mesh(mesh.devices.reshape(ZB, XB, CB, NPV), ("z", "x", "c", "views"))
    tiles = ("z", "x", "c")
    return jax.shard_map(
        on_device,
        mesh=fine,
        in_specs=(
            P(tiles, None, None),
            P(tiles, None, None, None),
            P(tiles, None, None),
            P(tiles, None),
            P(tiles, None),
            P(),
            P(),
            P(),
            P(),
            P(),
        ),
        out_specs=P(tiles, "views", None, None),
        check_vma=False,
    )
```

```python
import jax
import jax.numpy as jnp
import numpy as np
from jax import lax
from jax.experimental import pallas as pl
from jax.experimental.pallas import tpu as pltpu
from jax.sharding import Mesh, PartitionSpec as P

C = 32
G = 8
CH = 32
NDISP = 64
W = 128
NPV = 4
H = 8
LINE = 64
PIECE = 560
SLOTS = 55
PART = SLOTS * 16
BLOCKS = 18
ROWS = BLOCKS * 16
DL = 16
ZB, XB, CB = 8, 4, 2

bf16 = jnp.bfloat16
f32 = jnp.float32


def group_sum_matrix():
    table = np.zeros((256, 256), np.float32)
    for j in range(8):
        for ch in range(C):
            row, g = j * C + ch, ch // 4
            for b in range(3):
                table[row, b * 64 + j * G + g] = 1.0 / 16
                if j == 7:
                    table[row, 192 + b * 16 + g] = 1.0 / 16
                if j == 0:
                    table[row, 192 + b * 16 + 8 + g] = 1.0 / 16
    return np.concatenate([table, table], axis=0)


def spread_body(k1, k2, first, second):
    def repeat(cells, count):
        row = lax.broadcasted_iota(jnp.int32, (CH, count * CH), 0)
        lane = lax.broadcasted_iota(jnp.int32, (CH, count * CH), 1)
        copies = jnp.where((lane & 31) == row, 1.0, 0.0).astype(bf16)
        return jnp.dot(cells, copies, preferred_element_type=f32)

    wide1 = repeat(k1[...], 8)
    wide2 = repeat(k2[...], 8)
    lane1 = lax.broadcasted_iota(jnp.int32, (8, 256), 1) >> 5
    lane2 = lax.broadcasted_iota(jnp.int32, (CH, 256), 1) >> 5

    def line(cells, depth, a, b, j, col):
        result = jnp.zeros(col.shape, f32)
        for e in range(3):
            at = ((a * 3 + b) * 3 + e) * depth
            result = jnp.where(col == j + 1 - e, cells[at : at + depth], result)
        return result

    for a in range(3):
        for b in range(3):
            for j in range(0, 8, 2):
                pair = [line(wide1, G, a, b, j + i, lane1) for i in range(2)]
                first[a, b * 64 + j * 8 : b * 64 + j * 8 + 16, :] = jnp.concatenate(pair, 0).astype(bf16)
            pair = [line(wide1, G, a, b, j, lane1) for j in (-1, 8)]
            first[a, 192 + b * 16 : 208 + b * 16, :] = jnp.concatenate(pair, 0).astype(bf16)
            for j in range(8):
                at = b * 256 + j * 32
                second[a, at : at + 32, :] = line(wide2, CH, a, b, j, lane2).astype(bf16)
            for side, j in enumerate((-1, 8)):
                at = 768 + b * 64 + side * 32
                second[a, at : at + 32, :] = line(wide2, CH, a, b, j, lane2).astype(bf16)
        first[a, 240:256, :] = jnp.zeros((16, 256), bf16)
        second[a, 960:1024, :] = jnp.zeros((64, 256), bf16)


def spread_weights(k1, k2):
    return pl.pallas_call(
        spread_body,
        out_shape=(
            jax.ShapeDtypeStruct((3, 256, 256), bf16),
            jax.ShapeDtypeStruct((3, 1024, 256), bf16),
        ),
        name="spread_weights",
    )(k1.reshape(27 * G, CH), k2.reshape(27 * CH, CH))


def near(x):
    return pltpu.with_memory_space_constraint(x, pltpu.VMEM)


def merge_body(*refs):
    chunks, out, arrived = refs[:14], refs[14], refs[15]
    copies = []
    for spot, chunk in enumerate(chunks):
        at = spot * 2 * PIECE
        copies.append(pltpu.make_async_copy(chunk, out.at[at : at + 2 * PIECE], arrived.at[spot]))
        copies[-1].start()
    for copy in copies:
        copy.wait()


def merge_chunks(chunks):
    return pl.pallas_call(
        merge_body,
        out_shape=pltpu.VMEM((28 * PIECE, 128), bf16),
        compiler_params=pltpu.CompilerParams(vmem_limit_bytes=1 << 20),
        in_specs=[pl.BlockSpec(memory_space=pl.ANY)] * 14,
        out_specs=pl.BlockSpec(memory_space=pltpu.VMEM),
        scratch_shapes=[pltpu.SemaphoreType.DMA((14,))],
        name="merge_chunks",
    )(*chunks)


BUFFERS = 6


def select_body(links, where_am_i, *refs):
    early, late0, late1, out, stage, rows, tabs, listed = refs[:8]
    padded_all = refs[8 : 8 + BUFFERS]
    shifted_all = refs[8 + BUFFERS :]
    tau = where_am_i[0]
    core = where_am_i[1]
    view = where_am_i[2]
    here = where_am_i[3]

    def home(owner):
        dz = ((owner >> 3) - (here >> 3)) & 7
        dx = ((owner >> 1) - (here >> 1)) & 3
        turn = jnp.where(dx == 0, 0, jnp.where(dx == 3, 1, dx + 1))
        return (dz - (dz > 4).astype(jnp.int32)) * 4 + turn + jnp.where(dz == 4, 12, 0)

    def fetch(spot, extra, size):
        late = jnp.maximum(spot - 28, 0)
        near = pl.multiple_of(jnp.minimum(spot, 27) * PIECE + extra, 16)
        far = pl.multiple_of((late & 1) * PIECE + extra, 16)
        cells = jnp.where(late < 2, late0[pl.ds(far, size), :].astype(f32), late1[pl.ds(far, size), :].astype(f32))
        return jnp.where(spot < 28, early[pl.ds(near, size), :].astype(f32), cells)

    def look(tile, side):
        return jnp.where(tile >= 0, links[jnp.maximum(tile, 0) * 4 + side], -1)

    up, down, left, right = [links[tau * 4 + side] for side in range(4)]
    tiles = [
        [up, look(left, 0), look(right, 0)],
        [tau, left, right],
        [down, look(left, 1), look(right, 1)],
    ]
    for padded in padded_all:
        padded[0:8, :] = jnp.zeros((8, 128), f32)
        padded[72:88, :] = jnp.zeros((16, 128), f32)
    for slot in range(4 * SLOTS):
        stage[slot * 16 + 8 : slot * 16 + 16, :] = jnp.zeros((8, 128), f32)
        if slot % SLOTS >= 51:
            stage[slot * 16 : slot * 16 + 8, :] = jnp.zeros((8, 128), f32)
    lane = lax.broadcasted_iota(jnp.int32, (56, 128), 1)
    for spot in range(32):
        source = early if spot < 28 else (late0 if spot < 30 else late1)
        at = (spot if spot < 28 else spot & 1) * PIECE + 544
        cells = source[at : at + 16, :].astype(f32)
        rows[spot : spot + 1, :] = cells[8:9].astype(jnp.int32)
    listing = pltpu.make_async_copy(rows, tabs, listed)
    listing.start()
    listing.wait()

    def put_line(hh, band, column, number):
        padded, shifted = padded_all[number % BUFFERS], shifted_all[number % BUFFERS]
        source = tiles[band][column]
        row = hh - 2 if band == 1 else (6 + hh if band == 0 else hh - 10)
        known = jnp.maximum(source, 0)
        spot, column_at = home(known), (known & 1) * 24 + row
        owner = tabs[spot, column_at]
        index = tabs[spot, column_at + 8]
        start = tabs[spot, column_at + 16] + 2
        usable = (source >= 0) & ((owner & 1) == core)
        cells = fetch(home(owner), index * LINE, LINE)
        padded[8 : 8 + LINE, :] = jnp.where(usable, cells, 0.0)
        first = (start >> 2) + 7
        turn = (start & 3) * 32
        lower = padded[pl.ds(first, 56), :]
        upper = padded[pl.ds(first + 1, 56), :]
        shifted[...] = pltpu.roll(jnp.where(lane >= turn, lower, upper), (128 - turn) & 127, 1)
        for dest in range(4):
            begin = ((view + dest) & 3) * 4
            if column == 0:
                stage[pl.ds(dest * PART + hh, 37, 16), :] = shifted[pl.ds(begin, 37), :]
            elif column == 1:
                stage[pl.ds(dest * PART + 37 * 16 + hh, 7, 16), :] = shifted[pl.ds(begin + 30, 7), :]
            else:
                stage[pl.ds(dest * PART + 44 * 16 + hh, 7, 16), :] = shifted[pl.ds(begin, 7), :]

    for hh in range(12):
        for column in range(3):
            put_line(hh, 0 if hh < 2 else (1 if hh < 10 else 2), column, hh * 3 + column)

    above = view < 2
    halo = [jnp.where(above, tiles[0][k], tiles[2][k]) for k in range(3)]
    halo_row = jnp.where(above, view, view + 8)

    def features(tile, extra, size):
        cells = fetch(home(jnp.maximum(tile, 0)), extra, size)
        return jnp.where((tile >= 0) & ((tile & 1) == core), cells, 0.0)

    cells = features(halo[0], 512, 32)
    for dest in range(4):
        stage[pl.ds(dest * PART + 12 + view, 32, 16), :] = cells

    def put_pair(cells, slot, row):
        for dest in range(4):
            for k in range(2):
                stage[pl.ds(dest * PART + (slot + k) * 16 + row, 1), :] = cells[k : k + 1]

    put_pair(features(halo[1], 528, 16)[14:16], 51, halo_row)
    put_pair(features(halo[2], 512, 16)[0:2], 53, halo_row)
    left_cells = features(left, 544, 16)
    right_cells = features(right, 544, 16)
    for k in range(2):
        put_pair(left_cells[4 * k + 2 : 4 * k + 4], 51, 2 + 2 * view + k)
        put_pair(right_cells[4 * k : 4 * k + 2], 53, 2 + 2 * view + k)

    out[...] = stage[...].astype(bf16)


def select_pieces(links, where_am_i, early, late):
    return pl.pallas_call(
        select_body,
        out_shape=jax.ShapeDtypeStruct((4 * PART, 128), bf16),
        in_specs=[pl.BlockSpec(memory_space=pltpu.SMEM)] * 2 + [pl.BlockSpec(memory_space=pltpu.VMEM)] * 3,
        out_specs=pl.BlockSpec(memory_space=pltpu.VMEM),
        scratch_shapes=[
            pltpu.VMEM((4 * PART, 128), f32),
            pltpu.VMEM((32, 128), jnp.int32),
            pltpu.SMEM((32, 128), jnp.int32),
            pltpu.SemaphoreType.DMA,
        ]
        + [pltpu.VMEM((88, 128), f32)] * BUFFERS
        + [pltpu.VMEM((56, 128), f32)] * BUFFERS,
        compiler_params=pltpu.CompilerParams(vmem_limit_bytes=12 << 20),
        name="select_pieces",
    )(links, where_am_i, *[near(x) for x in (early, *late)])


def slot_of(block, half):
    if block == 0:
        return 37 + half
    if block == BLOCKS - 1:
        return 44 + half
    return 2 * (block - 1) + half


def volume_body(
    facts, band0, band1, band2, band3, ref, summing, first_bias, second_bias, first_far, second_far, out_far,
    turned, refx, factors, sums, padded, hidden, keep, wide, first, second, out, loaded, stored,
):
    first_copy = pltpu.make_async_copy(first_far, first, loaded.at[0])
    second_copy = pltpu.make_async_copy(second_far, second, loaded.at[1])
    first_copy.start()
    second_copy.start()
    view = facts[0]
    lane16 = lax.broadcasted_iota(jnp.int32, (16, 128), 1)
    sub8 = lax.broadcasted_iota(jnp.int32, (8, 128), 0)

    def total(slot):
        span = slice(slot * 16, slot * 16 + 16)
        return (band0[span, :].astype(f32) + band1[span, :].astype(f32)) + (
            band2[span, :].astype(f32) + band3[span, :].astype(f32)
        )

    lanes = [lane16 >= 32 * m for m in range(4)]
    current = total(0)
    for slot in range(51):
        following = total(slot + 1)
        turned[slot] = current
        for m in range(1, 4):
            turned[m * 51 + slot] = pltpu.roll(
                jnp.where(lanes[m], current, following), 128 - 32 * m, 1
            )
        if slot < 32:
            block, half = 1 + slot // 2, slot % 2
            halo = pltpu.roll(current[8:16], 4, 0)
            own = pltpu.roll(ref[:, slot * 128 : slot * 128 + 128].astype(f32), 2, 0)
            refx[block * 2 + half, 0:8] = jnp.where(sub8 < 2, halo, own)
            refx[block * 2 + half, 8:16] = jnp.where(sub8 < 2, own, halo)
        current = following
    for half in range(2):
        refx[half] = total(51 + half)
        refx[2 * (BLOCKS - 1) + half] = total(53 + half)

    row = lax.broadcasted_iota(jnp.int32, (ROWS, 128), 0)
    high, block = row & 15, row >> 4
    inside = (high >= jnp.where(facts[1] >= 0, 0, 1)) & (high <= jnp.where(facts[2] >= 0, 9, 8))
    inside &= (block >= jnp.where(facts[3] >= 0, 0, 1))
    inside &= (block <= jnp.where(facts[4] >= 0, BLOCKS - 1, BLOCKS - 2))
    keep[...] = jnp.where(inside, 1.0, 0.0)
    sums[ROWS:, :] = jnp.zeros((sums.shape[0] - ROWS, 256), f32)
    hidden[ROWS:, :] = jnp.zeros((hidden.shape[0] - ROWS, 256), f32)

    def cost_step(q, carry):
        for m in range(4):
            dd = 4 * q + m
            for block in range(BLOCKS):
                for half in range(2):
                    product = refx[2 * block + half] * turned[m * 51 + slot_of(block, half) + q]
                    top = product.astype(bf16)
                    rest = (product - top.astype(f32)).astype(bf16)
                    at = block * 16
                    factors[at : at + 16, half * 128 : half * 128 + 128] = top
                    factors[at : at + 16, 256 + half * 128 : 384 + half * 128] = rest
            cells = jnp.dot(factors[...], summing[...], preferred_element_type=f32)
            depth = 16 * view + dd - 2
            sums[0:ROWS, :] = jnp.where((depth >= 0) & (depth < NDISP), cells, 0.0)
            low = [
                [sums[block * 16 + b : block * 16 + b + 16, 128:256] for b in range(3)]
                for block in range(BLOCKS)
            ]
            mixed = [
                jnp.where(lane16 >= 96, cells[2], jnp.where(lane16 >= 80, cells[1], cells[0]))
                for cells in low
            ]
            from_right = (lane16 & 8) == 8
            for block in range(BLOCKS):
                at = block * 16
                head = jnp.where(lane16 < 64, sums[at : at + 16, 0:128], sums[at + 1 : at + 17, 0:128])
                edge = jnp.where(
                    from_right, mixed[min(block + 1, BLOCKS - 1)], mixed[max(block - 1, 0)]
                )
                tail = jnp.where(lane16 < 64, low[block][2], edge)
                line = pl.multiple_of(dd * ROWS + at, 16)
                padded[pl.ds(line, 16), 0:128] = head.astype(bf16)
                padded[pl.ds(line, 16), 128:256] = tail.astype(bf16)
        return carry

    lax.fori_loop(0, 5, cost_step, 0)

    lane8 = lax.broadcasted_iota(jnp.int32, (8, 128), 1)

    def hidden_step(step, carry):
        cells = jnp.broadcast_to(first_bias[...], (ROWS, 256))
        for a in range(3):
            at = pl.multiple_of((step + a) * ROWS, 16)
            cells = cells + jnp.dot(padded[pl.ds(at, ROWS), :], first[a], preferred_element_type=f32)
        depth = 16 * view + step - 1
        live = jnp.where((depth >= 0) & (depth < NDISP), keep[...], 0.0) > 0.5
        for part in range(2):
            span = slice(part * 128, part * 128 + 128)
            hidden[0:ROWS, span] = jnp.where(live, jnp.maximum(cells[:, span], 0.0), 0.0)

        def block_cells(block):
            at = block * 16
            parts, edges = [], []
            for b in range(3):
                parts.append(hidden[at + b : at + b + 8, 0:128])
                parts.append(hidden[at + b : at + b + 8, 128:256])
                before = hidden[at + b - 16 : at + b - 8, 128:256]
                after = hidden[at + b + 16 : at + b + 24, 0:128]
                edges.append(pltpu.roll(jnp.where(lane8 < 96, after, before), 96 if b == 1 else 32, 1))
            parts.append(jnp.where(lane8 < 64, edges[0], edges[1]))
            parts.append(edges[2])
            return parts

        for pair in range(8):
            one = block_cells(1 + 2 * pair)
            two = block_cells(2 + 2 * pair)
            at = pl.multiple_of(step * 128 + pair * 16, 16)
            for part in range(8):
                wide[pl.ds(at, 16), part * 128 : part * 128 + 128] = jnp.concatenate(
                    [one[part], two[part]], axis=0
                ).astype(bf16)
        return carry

    first_copy.wait()
    lax.fori_loop(0, DL + 2, hidden_step, 0)
    second_copy.wait()

    def stores(step):
        span = pl.ds(step * 4, 4)
        return pltpu.make_async_copy(out.at[span], out_far.at[span], stored.at[step])

    def output_step(step, carry):
        cells = jnp.broadcast_to(second_bias[...], (512, 256))
        for a in range(3):
            at = pl.multiple_of((step * 4 + a) * 128, 128)
            cells = cells + jnp.dot(wide[pl.ds(at, 512), :], second[a], preferred_element_type=f32)
        for d in range(4):
            for block in range(16):
                at = d * 128 + block * 8
                out[step * 4 + d, :, block * 256 : block * 256 + 256] = cells[at : at + 8, :]
        stores(step).start()
        return carry

    lax.fori_loop(0, 4, output_step, 0)
    for step in range(4):
        stores(step).wait()


def volume(facts, bands, ref, first, first_bias, second, second_bias):
    operands = (
        facts, *[near(band) for band in bands], ref, jnp.asarray(group_sum_matrix(), bf16),
        first_bias, second_bias,
    )
    return pl.pallas_call(
        volume_body,
        out_shape=jax.ShapeDtypeStruct((DL, H, W * CH), f32),
        in_specs=[pl.BlockSpec(memory_space=pltpu.SMEM)]
        + [pl.BlockSpec(memory_space=pltpu.VMEM)] * 8
        + [pl.BlockSpec(memory_space=pl.ANY)] * 2,
        out_specs=pl.BlockSpec(memory_space=pl.ANY),
        scratch_shapes=[
            pltpu.VMEM((4 * 51, 16, 128), f32),
            pltpu.VMEM((2 * BLOCKS, 16, 128), f32),
            pltpu.VMEM((ROWS, 512), bf16),
            pltpu.VMEM((ROWS + 16, 256), f32),
            pltpu.VMEM((20 * ROWS, 256), bf16),
            pltpu.VMEM((ROWS + 16, 256), f32),
            pltpu.VMEM((ROWS, 128), f32),
            pltpu.VMEM((18 * 128, 1024), bf16),
            pltpu.VMEM(first.shape, bf16),
            pltpu.VMEM(second.shape, bf16),
            pltpu.VMEM((DL, H, W * CH), f32),
            pltpu.SemaphoreType.DMA((2,)),
            pltpu.SemaphoreType.DMA((4,)),
        ],
        compiler_params=pltpu.CompilerParams(vmem_limit_bytes=48 << 20),
        name="volume",
    )(*operands, first, second)


def on_device(
    ref_features, partner_lines, line_owner, line_index, line_offset, neighbours,
    conv1_weight, conv1_bias, conv2_weight, conv2_bias,
):
    view = lax.axis_index("views")
    core = lax.axis_index("c")
    tile = (lax.axis_index("z") * XB + lax.axis_index("x")) * CB + core
    ref = ref_features[0]

    lines = lax.dynamic_index_in_dim(partner_lines[0], view, 0, keepdims=False)
    halo_row = lax.dynamic_slice_in_dim(ref, (view + 6) % 8, 1, axis=0)
    sides = lax.dynamic_slice_in_dim(ref, 2 * view, 2, axis=0)
    sides = jnp.concatenate([sides[:, 0:256], sides[:, 3840:4096]], axis=1)
    names = jnp.stack([line_owner[0, :, 0], line_index[0], line_offset[0]])
    names = lax.dynamic_slice_in_dim(names, view * 8, 8, axis=1).astype(bf16).reshape(24)
    twin = lax.ppermute(names, "c", [(0, 1), (1, 0)])
    names = jnp.where(core == 0, jnp.concatenate([names, twin]), jnp.concatenate([twin, names]))
    payload = jnp.concatenate(
        [
            lines.reshape(8 * LINE, 128),
            halo_row.reshape(32, 128),
            sides.reshape(8, 128),
            jnp.pad(names[None], ((0, 7), (0, 80))),
        ],
        axis=0,
    )
    def shift(x, axis, by):
        count = lax.axis_size(axis)
        return lax.ppermute(x, axis, [(i, (i + by) % count) for i in range(count)])

    one, two, three = shift(payload, "x", 1), shift(payload, "x", -1), shift(payload, "x", 2)
    chunks = [[None, None] for _ in range(8)]
    chunks[0] = [jnp.concatenate([payload, one]), jnp.concatenate([two, three])]
    for k in range(1, 4):
        for i in range(2):
            chunks[-k % 8][i] = shift(chunks[(1 - k) % 8][i], "z", 1)
            chunks[k][i] = shift(chunks[k - 1][i], "z", -1)
    last = [shift(chunks[5][0], "z", 1), shift(chunks[3][1], "z", -1)]
    early = merge_chunks([chunk for k in range(8) if k != 4 for chunk in chunks[k]])

    links = neighbours.reshape(256)

    first, second = spread_weights(conv1_weight, conv2_weight)
    first_bias = jnp.tile(conv1_bias, 8)[None]
    second_bias = jnp.tile(conv2_bias, 8)[None]
    facts = jnp.concatenate([view[None], neighbours[tile]])
    other = tile + 1 - 2 * core
    asked = jnp.stack([other, core, view, tile])
    wanted = jnp.stack([tile, core, view, tile])
    links, asked, wanted, first, second, first_bias, second_bias, facts = lax.optimization_barrier(
        (links, asked, wanted, first, second, first_bias, second_bias, facts)
    )
    theirs = select_pieces(links, asked, early, last)
    swapped = lax.ppermute(theirs, "c", [(0, 1), (1, 0)])
    own = select_pieces(links, wanted, early, last)

    def part(step):
        span = slice(step * PART, (step + 1) * PART)
        return own[span] + swapped[span]

    bands = [part(0)] + [shift(part(step), "views", step) for step in (1, 2, 3)]
    return volume(facts, bands, ref, first, first_bias, second, second_bias)[None]


def solution(mesh):
    fine = Mesh(mesh.devices.reshape(ZB, XB, CB, NPV), ("z", "x", "c", "views"))
    tiles = ("z", "x", "c")
    return jax.shard_map(
        on_device,
        mesh=fine,
        in_specs=(
            P(tiles, None, None),
            P(tiles, None, None, None),
            P(tiles, None, None),
            P(tiles, None),
            P(tiles, None),
            P(),
            P(),
            P(),
            P(),
            P(),
        ),
        out_specs=P(tiles, "views", None, None),
        check_vma=False,
    )
```

```python
import jax
import jax.numpy as jnp
import numpy as np
from jax import lax
from jax.experimental import pallas as pl
from jax.experimental.pallas import tpu as pltpu
from jax.sharding import Mesh, PartitionSpec as P


C = 32
G = 8
CH = 32
NDISP = 64
W = 128
NPV = 4
H = 8
LINE = 64
PIECE = 560
SLOTS = 55
PART = SLOTS * 16
BLOCKS = 18
ROWS = BLOCKS * 16
DL = 16
HALF = 28
ZB, XB, CB = 8, 4, 2

bf16 = jnp.bfloat16
f32 = jnp.float32


def group_sum_matrix():
    table = np.zeros((256, 256), np.float32)
    for j in range(8):
        for ch in range(C):
            row, g = j * C + ch, ch // 4
            for b in range(3):
                table[row, b * 64 + j * G + g] = 1.0 / 16
                if j == 7:
                    table[row, 192 + b * 16 + g] = 1.0 / 16
                if j == 0:
                    table[row, 192 + b * 16 + 8 + g] = 1.0 / 16
    return np.concatenate([table, table], axis=0)


def spread_body(k1, k2, first, second):
    def repeat(cells, count):
        row = lax.broadcasted_iota(jnp.int32, (CH, count * CH), 0)
        lane = lax.broadcasted_iota(jnp.int32, (CH, count * CH), 1)
        copies = jnp.where((lane & 31) == row, 1.0, 0.0).astype(bf16)
        return jnp.dot(cells, copies, preferred_element_type=f32)

    wide1 = repeat(k1[...], 8)
    wide2 = repeat(k2[...], 8)
    lane1 = lax.broadcasted_iota(jnp.int32, (8, 256), 1) >> 5
    lane2 = lax.broadcasted_iota(jnp.int32, (CH, 256), 1) >> 5

    def line(cells, depth, a, b, j, col):
        result = jnp.zeros(col.shape, f32)
        for e in range(3):
            at = ((a * 3 + b) * 3 + e) * depth
            result = jnp.where(col == j + 1 - e, cells[at : at + depth], result)
        return result

    for a in range(3):
        for b in range(3):
            for j in range(0, 8, 2):
                pair = [line(wide1, G, a, b, j + i, lane1) for i in range(2)]
                first[a, b * 64 + j * 8 : b * 64 + j * 8 + 16, :] = jnp.concatenate(pair, 0).astype(bf16)
            pair = [line(wide1, G, a, b, j, lane1) for j in (-1, 8)]
            first[a, 192 + b * 16 : 208 + b * 16, :] = jnp.concatenate(pair, 0).astype(bf16)
            for j in range(8):
                at = b * 256 + j * 32
                second[a, at : at + 32, :] = line(wide2, CH, a, b, j, lane2).astype(bf16)
            for side, j in enumerate((-1, 8)):
                at = 768 + b * 64 + side * 32
                second[a, at : at + 32, :] = line(wide2, CH, a, b, j, lane2).astype(bf16)
        first[a, 240:256, :] = jnp.zeros((16, 256), bf16)
        second[a, 960:1024, :] = jnp.zeros((64, 256), bf16)


def spread_weights(k1, k2):
    return pl.pallas_call(
        spread_body,
        out_shape=(
            jax.ShapeDtypeStruct((3, 256, 256), bf16),
            jax.ShapeDtypeStruct((3, 1024, 256), bf16),
        ),
        name="spread_weights",
    )(k1.reshape(27 * G, CH), k2.reshape(27 * CH, CH))


def near(x):
    return pltpu.with_memory_space_constraint(x, pltpu.VMEM)


def merge_body(*refs):
    chunks, out, arrived = refs[:14], refs[14], refs[15]
    copies = []
    for spot, chunk in enumerate(chunks):
        at = spot * 2 * PIECE
        copies.append(pltpu.make_async_copy(chunk, out.at[at : at + 2 * PIECE], arrived.at[spot]))
        copies[-1].start()
    for copy in copies:
        copy.wait()


def merge_chunks(chunks):
    return pl.pallas_call(
        merge_body,
        out_shape=pltpu.VMEM((28 * PIECE, 128), bf16),
        compiler_params=pltpu.CompilerParams(vmem_limit_bytes=1 << 20),
        in_specs=[pl.BlockSpec(memory_space=pl.ANY)] * 14,
        out_specs=pl.BlockSpec(memory_space=pltpu.VMEM),
        scratch_shapes=[pltpu.SemaphoreType.DMA((14,))],
        name="merge_chunks",
    )(*chunks)


BUFFERS = 6


def select_body(links, where_am_i, *refs):
    early, late0, late1, out, stage, rows, tabs, listed = refs[:8]
    padded_all = refs[8 : 8 + BUFFERS]
    shifted_all = refs[8 + BUFFERS :]
    tau = where_am_i[0]
    core = where_am_i[1]
    view = where_am_i[2]
    here = where_am_i[3]

    def home(owner):
        dz = ((owner >> 3) - (here >> 3)) & 7
        dx = ((owner >> 1) - (here >> 1)) & 3
        turn = jnp.where(dx == 0, 0, jnp.where(dx == 3, 1, dx + 1))
        return (dz - (dz > 4).astype(jnp.int32)) * 4 + turn + jnp.where(dz == 4, 12, 0)

    def fetch(spot, extra, size):
        late = jnp.maximum(spot - 28, 0)
        near = pl.multiple_of(jnp.minimum(spot, 27) * PIECE + extra, 16)
        far = pl.multiple_of((late & 1) * PIECE + extra, 16)
        cells = jnp.where(late < 2, late0[pl.ds(far, size), :].astype(f32), late1[pl.ds(far, size), :].astype(f32))
        return jnp.where(spot < 28, early[pl.ds(near, size), :].astype(f32), cells)

    def look(tile, side):
        return jnp.where(tile >= 0, links[jnp.maximum(tile, 0) * 4 + side], -1)

    up, down, left, right = [links[tau * 4 + side] for side in range(4)]
    tiles = [
        [up, look(left, 0), look(right, 0)],
        [tau, left, right],
        [down, look(left, 1), look(right, 1)],
    ]
    for padded in padded_all:
        padded[0:8, :] = jnp.zeros((8, 128), f32)
        padded[72:88, :] = jnp.zeros((16, 128), f32)
    for slot in range(4 * SLOTS):
        stage[slot * 16 + 8 : slot * 16 + 16, :] = jnp.zeros((8, 128), f32)
        if slot % SLOTS >= 51:
            stage[slot * 16 : slot * 16 + 8, :] = jnp.zeros((8, 128), f32)
    lane = lax.broadcasted_iota(jnp.int32, (56, 128), 1)
    for spot in range(32):
        source = early if spot < 28 else (late0 if spot < 30 else late1)
        at = (spot if spot < 28 else spot & 1) * PIECE + 544
        cells = source[at : at + 16, :].astype(f32)
        rows[spot : spot + 1, :] = cells[8:9].astype(jnp.int32)
    listing = pltpu.make_async_copy(rows, tabs, listed)
    listing.start()
    listing.wait()

    def put_line(hh, band, column, number):
        padded, shifted = padded_all[number % BUFFERS], shifted_all[number % BUFFERS]
        source = tiles[band][column]
        row = hh - 2 if band == 1 else (6 + hh if band == 0 else hh - 10)
        known = jnp.maximum(source, 0)
        spot, column_at = home(known), (known & 1) * 24 + row
        owner = tabs[spot, column_at]
        index = tabs[spot, column_at + 8]
        start = tabs[spot, column_at + 16] + 2
        usable = (source >= 0) & ((owner & 1) == core)
        cells = fetch(home(owner), index * LINE, LINE)
        padded[8 : 8 + LINE, :] = jnp.where(usable, cells, 0.0)
        first = (start >> 2) + 7
        turn = (start & 3) * 32
        lower = padded[pl.ds(first, 56), :]
        upper = padded[pl.ds(first + 1, 56), :]
        shifted[...] = pltpu.roll(jnp.where(lane >= turn, lower, upper), (128 - turn) & 127, 1)
        for dest in range(4):
            begin = ((view + dest) & 3) * 4
            if column == 0:
                stage[pl.ds(dest * PART + hh, 37, 16), :] = shifted[pl.ds(begin, 37), :]
            elif column == 1:
                stage[pl.ds(dest * PART + 37 * 16 + hh, 7, 16), :] = shifted[pl.ds(begin + 30, 7), :]
            else:
                stage[pl.ds(dest * PART + 44 * 16 + hh, 7, 16), :] = shifted[pl.ds(begin, 7), :]

    for hh in range(12):
        for column in range(3):
            put_line(hh, 0 if hh < 2 else (1 if hh < 10 else 2), column, hh * 3 + column)

    above = view < 2
    halo = [jnp.where(above, tiles[0][k], tiles[2][k]) for k in range(3)]
    halo_row = jnp.where(above, view, view + 8)

    def features(tile, extra, size):
        cells = fetch(home(jnp.maximum(tile, 0)), extra, size)
        return jnp.where((tile >= 0) & ((tile & 1) == core), cells, 0.0)

    cells = features(halo[0], 512, 32)
    for dest in range(4):
        stage[pl.ds(dest * PART + 12 + view, 32, 16), :] = cells

    def put_pair(cells, slot, row):
        for dest in range(4):
            for k in range(2):
                stage[pl.ds(dest * PART + (slot + k) * 16 + row, 1), :] = cells[k : k + 1]

    put_pair(features(halo[1], 528, 16)[14:16], 51, halo_row)
    put_pair(features(halo[2], 512, 16)[0:2], 53, halo_row)
    left_cells = features(left, 544, 16)
    right_cells = features(right, 544, 16)
    for k in range(2):
        put_pair(left_cells[4 * k + 2 : 4 * k + 4], 51, 2 + 2 * view + k)
        put_pair(right_cells[4 * k : 4 * k + 2], 53, 2 + 2 * view + k)

    out[...] = stage[...].astype(bf16)


def select_pieces(links, where_am_i, early, late):
    return pl.pallas_call(
        select_body,
        out_shape=jax.ShapeDtypeStruct((4 * PART, 128), bf16),
        in_specs=[pl.BlockSpec(memory_space=pltpu.SMEM)] * 2 + [pl.BlockSpec(memory_space=pltpu.VMEM)] * 3,
        out_specs=pl.BlockSpec(memory_space=pltpu.VMEM),
        scratch_shapes=[
            pltpu.VMEM((4 * PART, 128), f32),
            pltpu.VMEM((32, 128), jnp.int32),
            pltpu.SMEM((32, 128), jnp.int32),
            pltpu.SemaphoreType.DMA,
        ]
        + [pltpu.VMEM((88, 128), f32)] * BUFFERS
        + [pltpu.VMEM((56, 128), f32)] * BUFFERS,
        compiler_params=pltpu.CompilerParams(vmem_limit_bytes=12 << 20),
        name="select_pieces",
    )(links, where_am_i, *[near(x) for x in (early, *late)])


def slot_of(block, half):
    if block == 0:
        return 37 + half
    if block == BLOCKS - 1:
        return 44 + half
    return 2 * (block - 1) + half


def volume_body(
    facts, band0, band1, band2, band3, band4, ref, summing, first_bias, second_bias, first_far, second_far, out_far,
    turned, refx, factors, sums, padded, hidden, keep, wide, first, second, out, loaded, stored,
):
    first_copy = pltpu.make_async_copy(first_far, first, loaded.at[0])
    second_copy = pltpu.make_async_copy(second_far, second, loaded.at[1])
    first_copy.start()
    second_copy.start()
    view = facts[0]
    lane16 = lax.broadcasted_iota(jnp.int32, (16, 128), 1)
    sub8 = lax.broadcasted_iota(jnp.int32, (8, 128), 0)

    def total(slot):
        span = slice(slot * 16, slot * 16 + 16)
        if slot < HALF:
            opposite = band2[span, :].astype(f32)
        else:
            opposite = band4[slot * 16 - HALF * 16 : slot * 16 - HALF * 16 + 16, :].astype(f32)
        return (band0[span, :].astype(f32) + band1[span, :].astype(f32)) + (
            opposite + band3[span, :].astype(f32)
        )

    lanes = [lane16 >= 32 * m for m in range(4)]
    current = total(0)
    for slot in range(51):
        following = total(slot + 1)
        turned[slot] = current
        for m in range(1, 4):
            turned[m * 51 + slot] = pltpu.roll(
                jnp.where(lanes[m], current, following), 128 - 32 * m, 1
            )
        if slot < 32:
            block, half = 1 + slot // 2, slot % 2
            halo = pltpu.roll(current[8:16], 4, 0)
            own = pltpu.roll(ref[:, slot * 128 : slot * 128 + 128].astype(f32), 2, 0)
            refx[block * 2 + half, 0:8] = jnp.where(sub8 < 2, halo, own)
            refx[block * 2 + half, 8:16] = jnp.where(sub8 < 2, own, halo)
        current = following
    for half in range(2):
        refx[half] = total(51 + half)
        refx[2 * (BLOCKS - 1) + half] = total(53 + half)

    row = lax.broadcasted_iota(jnp.int32, (ROWS, 128), 0)
    high, block = row & 15, row >> 4
    inside = (high >= jnp.where(facts[1] >= 0, 0, 1)) & (high <= jnp.where(facts[2] >= 0, 9, 8))
    inside &= (block >= jnp.where(facts[3] >= 0, 0, 1))
    inside &= (block <= jnp.where(facts[4] >= 0, BLOCKS - 1, BLOCKS - 2))
    keep[...] = jnp.where(inside, 1.0, 0.0)
    sums[ROWS:, :] = jnp.zeros((sums.shape[0] - ROWS, 256), f32)
    hidden[ROWS:, :] = jnp.zeros((hidden.shape[0] - ROWS, 256), f32)

    def cost_step(q, carry):
        for m in range(4):
            dd = 4 * q + m
            for block in range(BLOCKS):
                for half in range(2):
                    product = refx[2 * block + half] * turned[m * 51 + slot_of(block, half) + q]
                    top = product.astype(bf16)
                    rest = (product - top.astype(f32)).astype(bf16)
                    at = block * 16
                    factors[at : at + 16, half * 128 : half * 128 + 128] = top
                    factors[at : at + 16, 256 + half * 128 : 384 + half * 128] = rest
            cells = jnp.dot(factors[...], summing[...], preferred_element_type=f32)
            depth = 16 * view + dd - 2
            sums[0:ROWS, :] = jnp.where((depth >= 0) & (depth < NDISP), cells, 0.0)
            from_right = (lane16 & 8) == 8

            def mixed_cells(block):
                low = [sums[block * 16 + b : block * 16 + b + 16, 128:256] for b in range(3)]
                return low[2], jnp.where(lane16 >= 96, low[2], jnp.where(lane16 >= 80, low[1], low[0]))

            this_low, this_mixed = mixed_cells(0)
            last_mixed = this_mixed
            for block in range(BLOCKS):
                at = block * 16
                next_low, next_mixed = mixed_cells(min(block + 1, BLOCKS - 1))
                head = jnp.where(lane16 < 64, sums[at : at + 16, 0:128], sums[at + 1 : at + 17, 0:128])
                edge = jnp.where(from_right, next_mixed, last_mixed)
                tail = jnp.where(lane16 < 64, this_low, edge)
                line = pl.multiple_of(dd * ROWS + at, 16)
                padded[pl.ds(line, 16), 0:128] = head.astype(bf16)
                padded[pl.ds(line, 16), 128:256] = tail.astype(bf16)
                this_low, last_mixed, this_mixed = next_low, this_mixed, next_mixed
        return carry

    lax.fori_loop(0, 5, cost_step, 0)

    lane8 = lax.broadcasted_iota(jnp.int32, (8, 128), 1)

    def hidden_step(step, carry):
        cells = jnp.broadcast_to(first_bias[...], (ROWS, 256))
        for a in range(3):
            at = pl.multiple_of((step + a) * ROWS, 16)
            cells = cells + jnp.dot(padded[pl.ds(at, ROWS), :], first[a], preferred_element_type=f32)
        depth = 16 * view + step - 1
        live = jnp.where((depth >= 0) & (depth < NDISP), keep[...], 0.0) > 0.5
        for part in range(2):
            span = slice(part * 128, part * 128 + 128)
            hidden[0:ROWS, span] = jnp.where(live, jnp.maximum(cells[:, span], 0.0), 0.0)

        def block_cells(block):
            at = block * 16
            parts, edges = [], []
            for b in range(3):
                parts.append(hidden[at + b : at + b + 8, 0:128])
                parts.append(hidden[at + b : at + b + 8, 128:256])
                before = hidden[at + b - 16 : at + b - 8, 128:256]
                after = hidden[at + b + 16 : at + b + 24, 0:128]
                edges.append(pltpu.roll(jnp.where(lane8 < 96, after, before), 96 if b == 1 else 32, 1))
            parts.append(jnp.where(lane8 < 64, edges[0], edges[1]))
            parts.append(edges[2])
            return parts

        for pair in range(8):
            one = block_cells(1 + 2 * pair)
            two = block_cells(2 + 2 * pair)
            at = pl.multiple_of(step * 128 + pair * 16, 16)
            for part in range(8):
                wide[pl.ds(at, 16), part * 128 : part * 128 + 128] = jnp.concatenate(
                    [one[part], two[part]], axis=0
                ).astype(bf16)
        return carry

    first_copy.wait()
    lax.fori_loop(0, DL + 2, hidden_step, 0)
    second_copy.wait()

    def stores(step):
        span = pl.ds(step * 4, 4)
        return pltpu.make_async_copy(out.at[span], out_far.at[span], stored.at[step])

    def output_step(step, carry):
        cells = jnp.broadcast_to(second_bias[...], (512, 256))
        for a in range(3):
            at = pl.multiple_of((step * 4 + a) * 128, 128)
            cells = cells + jnp.dot(wide[pl.ds(at, 512), :], second[a], preferred_element_type=f32)
        for d in range(4):
            for block in range(16):
                at = d * 128 + block * 8
                out[step * 4 + d, :, block * 256 : block * 256 + 256] = cells[at : at + 8, :]
        stores(step).start()
        return carry

    lax.fori_loop(0, 4, output_step, 0)
    for step in range(4):
        stores(step).wait()


def volume(facts, bands, ref, first, first_bias, second, second_bias):
    operands = (
        facts, *[near(band) for band in bands], ref, jnp.asarray(group_sum_matrix(), bf16),
        first_bias, second_bias,
    )
    return pl.pallas_call(
        volume_body,
        out_shape=jax.ShapeDtypeStruct((DL, H, W * CH), f32),
        in_specs=[pl.BlockSpec(memory_space=pltpu.SMEM)]
        + [pl.BlockSpec(memory_space=pltpu.VMEM)] * 9
        + [pl.BlockSpec(memory_space=pl.ANY)] * 2,
        out_specs=pl.BlockSpec(memory_space=pl.ANY),
        scratch_shapes=[
            pltpu.VMEM((4 * 51, 16, 128), f32),
            pltpu.VMEM((2 * BLOCKS, 16, 128), f32),
            pltpu.VMEM((ROWS, 512), bf16),
            pltpu.VMEM((ROWS + 16, 256), f32),
            pltpu.VMEM((20 * ROWS, 256), bf16),
            pltpu.VMEM((ROWS + 16, 256), f32),
            pltpu.VMEM((ROWS, 128), f32),
            pltpu.VMEM((18 * 128, 1024), bf16),
            pltpu.VMEM(first.shape, bf16),
            pltpu.VMEM(second.shape, bf16),
            pltpu.VMEM((DL, H, W * CH), f32),
            pltpu.SemaphoreType.DMA((2,)),
            pltpu.SemaphoreType.DMA((4,)),
        ],
        compiler_params=pltpu.CompilerParams(vmem_limit_bytes=48 << 20),
        name="volume",
    )(*operands, first, second)


def on_device(
    ref_features, partner_lines, line_owner, line_index, line_offset, neighbours,
    conv1_weight, conv1_bias, conv2_weight, conv2_bias,
):
    view = lax.axis_index("views")
    core = lax.axis_index("c")
    tile = (lax.axis_index("z") * XB + lax.axis_index("x")) * CB + core
    ref = ref_features[0]

    lines = lax.dynamic_index_in_dim(partner_lines[0], view, 0, keepdims=False)
    halo_row = lax.dynamic_slice_in_dim(ref, (view + 6) % 8, 1, axis=0)
    sides = lax.dynamic_slice_in_dim(ref, 2 * view, 2, axis=0)
    sides = jnp.concatenate([sides[:, 0:256], sides[:, 3840:4096]], axis=1)
    names = jnp.stack([line_owner[0, :, 0], line_index[0], line_offset[0]])
    names = lax.dynamic_slice_in_dim(names, view * 8, 8, axis=1).astype(bf16).reshape(24)
    twin = lax.ppermute(names, "c", [(0, 1), (1, 0)])
    names = jnp.where(core == 0, jnp.concatenate([names, twin]), jnp.concatenate([twin, names]))
    payload = jnp.concatenate(
        [
            lines.reshape(8 * LINE, 128),
            halo_row.reshape(32, 128),
            sides.reshape(8, 128),
            jnp.pad(names[None], ((0, 7), (0, 80))),
        ],
        axis=0,
    )

    def shift(x, axis, by):
        count = lax.axis_size(axis)
        return lax.ppermute(x, axis, [(i, (i + by) % count) for i in range(count)])

    one, two, three = shift(payload, "x", 1), shift(payload, "x", -1), shift(payload, "x", 2)
    chunks = [[None, None] for _ in range(8)]
    chunks[0] = [jnp.concatenate([payload, one]), jnp.concatenate([two, three])]
    for k in range(1, 4):
        for i in range(2):
            chunks[-k % 8][i] = shift(chunks[(1 - k) % 8][i], "z", 1)
            chunks[k][i] = shift(chunks[k - 1][i], "z", -1)
    last = [shift(chunks[5][0], "z", 1), shift(chunks[3][1], "z", -1)]
    early = merge_chunks([chunk for k in range(8) if k != 4 for chunk in chunks[k]])

    links = neighbours.reshape(256)

    first, second = spread_weights(conv1_weight, conv2_weight)
    first_bias = jnp.tile(conv1_bias, 8)[None]
    second_bias = jnp.tile(conv2_bias, 8)[None]
    facts = jnp.concatenate([view[None], neighbours[tile]])
    other = tile + 1 - 2 * core
    asked = jnp.stack([other, core, view, tile])
    wanted = jnp.stack([tile, core, view, tile])
    links, asked, wanted, first, second, first_bias, second_bias, facts = lax.optimization_barrier(
        (links, asked, wanted, first, second, first_bias, second_bias, facts)
    )
    theirs = select_pieces(links, asked, early, last)
    swapped = lax.ppermute(theirs, "c", [(0, 1), (1, 0)])
    own = select_pieces(links, wanted, early, last)

    def part(begin, end):
        return own[begin:end] + swapped[begin:end]

    middle = 2 * PART + HALF * 16
    upward = shift(part(2 * PART, middle), "views", 1)
    downward = shift(part(middle, 3 * PART), "views", -1)
    bands = [
        part(0, PART),
        shift(part(PART, 2 * PART), "views", 1),
        shift(upward, "views", 1),
        shift(part(3 * PART, 4 * PART), "views", -1),
        shift(downward, "views", -1),
    ]
    return volume(facts, bands, ref, first, first_bias, second, second_bias)[None]


def solution(mesh):
    fine = Mesh(mesh.devices.reshape(ZB, XB, CB, NPV), ("z", "x", "c", "views"))
    tiles = ("z", "x", "c")
    return jax.shard_map(
        on_device,
        mesh=fine,
        in_specs=(
            P(tiles, None, None),
            P(tiles, None, None, None),
            P(tiles, None, None),
            P(tiles, None),
            P(tiles, None),
            P(),
            P(),
            P(),
            P(),
            P(),
        ),
        out_specs=P(tiles, "views", None, None),
        check_vma=False,
    )
```

```python
import jax
import jax.numpy as jnp
import numpy as np
from jax import lax
from jax.experimental import pallas as pl
from jax.experimental.pallas import tpu as pltpu
from jax.sharding import Mesh, PartitionSpec as P


C = 32
G = 8
CH = 32
NDISP = 64
W = 128
NPV = 4
H = 8
LINE = 64
PIECE = 560
SLOTS = 55
PART = SLOTS * 16
BLOCKS = 18
ROWS = BLOCKS * 16
DL = 16
HALF = 28
ZB, XB, CB = 8, 4, 2

bf16 = jnp.bfloat16
f32 = jnp.float32


def group_sum_matrix():
    table = np.zeros((256, 256), np.float32)
    for j in range(8):
        for ch in range(C):
            row, g = j * C + ch, ch // 4
            for b in range(3):
                table[row, b * 64 + j * G + g] = 1.0 / 16
                if j == 7:
                    table[row, 192 + b * 16 + g] = 1.0 / 16
                if j == 0:
                    table[row, 192 + b * 16 + 8 + g] = 1.0 / 16
    return np.concatenate([table, table], axis=0)


def spread_body(k1, k2, first, second):
    def repeat(cells, count):
        row = lax.broadcasted_iota(jnp.int32, (CH, count * CH), 0)
        lane = lax.broadcasted_iota(jnp.int32, (CH, count * CH), 1)
        copies = jnp.where((lane & 31) == row, 1.0, 0.0).astype(bf16)
        return jnp.dot(cells, copies, preferred_element_type=f32)

    wide1 = repeat(k1[...], 8)
    wide2 = repeat(k2[...], 8)
    lane1 = lax.broadcasted_iota(jnp.int32, (8, 256), 1) >> 5
    lane2 = lax.broadcasted_iota(jnp.int32, (CH, 256), 1) >> 5

    def line(cells, depth, a, b, j, col):
        result = jnp.zeros(col.shape, f32)
        for e in range(3):
            at = ((a * 3 + b) * 3 + e) * depth
            result = jnp.where(col == j + 1 - e, cells[at : at + depth], result)
        return result

    for a in range(3):
        for b in range(3):
            for j in range(0, 8, 2):
                pair = [line(wide1, G, a, b, j + i, lane1) for i in range(2)]
                first[a, b * 64 + j * 8 : b * 64 + j * 8 + 16, :] = jnp.concatenate(pair, 0).astype(bf16)
            pair = [line(wide1, G, a, b, j, lane1) for j in (-1, 8)]
            first[a, 192 + b * 16 : 208 + b * 16, :] = jnp.concatenate(pair, 0).astype(bf16)
            for j in range(8):
                at = b * 256 + j * 32
                second[a, at : at + 32, :] = line(wide2, CH, a, b, j, lane2).astype(bf16)
            for side, j in enumerate((-1, 8)):
                at = 768 + b * 64 + side * 32
                second[a, at : at + 32, :] = line(wide2, CH, a, b, j, lane2).astype(bf16)
        first[a, 240:256, :] = jnp.zeros((16, 256), bf16)
        second[a, 960:1024, :] = jnp.zeros((64, 256), bf16)


def spread_weights(k1, k2):
    return pl.pallas_call(
        spread_body,
        out_shape=(
            jax.ShapeDtypeStruct((3, 256, 256), bf16),
            jax.ShapeDtypeStruct((3, 1024, 256), bf16),
        ),
        name="spread_weights",
    )(k1.reshape(27 * G, CH), k2.reshape(27 * CH, CH))


def near(x):
    return pltpu.with_memory_space_constraint(x, pltpu.VMEM)


def merge_body(*refs):
    chunks, out, arrived = refs[:14], refs[14], refs[15]
    copies = []
    for spot, chunk in enumerate(chunks):
        at = spot * 2 * PIECE
        copies.append(pltpu.make_async_copy(chunk, out.at[at : at + 2 * PIECE], arrived.at[spot]))
        copies[-1].start()
    for copy in copies:
        copy.wait()


def merge_chunks(chunks):
    return pl.pallas_call(
        merge_body,
        out_shape=pltpu.VMEM((28 * PIECE, 128), bf16),
        compiler_params=pltpu.CompilerParams(vmem_limit_bytes=1 << 20),
        in_specs=[pl.BlockSpec(memory_space=pl.ANY)] * 14,
        out_specs=pl.BlockSpec(memory_space=pltpu.VMEM),
        scratch_shapes=[pltpu.SemaphoreType.DMA((14,))],
        name="merge_chunks",
    )(*chunks)


BUFFERS = 6


def select_body(links, where_am_i, *refs):
    early, late0, late1, out, stage, rows, tabs, listed = refs[:8]
    padded_all = refs[8 : 8 + BUFFERS]
    shifted_all = refs[8 + BUFFERS :]
    tau = where_am_i[0]
    core = where_am_i[1]
    view = where_am_i[2]
    here = where_am_i[3]

    def home(owner):
        dz = ((owner >> 3) - (here >> 3)) & 7
        dx = ((owner >> 1) - (here >> 1)) & 3
        turn = jnp.where(dx == 0, 0, jnp.where(dx == 3, 1, dx + 1))
        return (dz - (dz > 4).astype(jnp.int32)) * 4 + turn + jnp.where(dz == 4, 12, 0)

    def fetch(spot, extra, size):
        late = jnp.maximum(spot - 28, 0)
        near = pl.multiple_of(jnp.minimum(spot, 27) * PIECE + extra, 16)
        far = pl.multiple_of((late & 1) * PIECE + extra, 16)
        cells = jnp.where(late < 2, late0[pl.ds(far, size), :].astype(f32), late1[pl.ds(far, size), :].astype(f32))
        return jnp.where(spot < 28, early[pl.ds(near, size), :].astype(f32), cells)

    def look(tile, side):
        return jnp.where(tile >= 0, links[jnp.maximum(tile, 0) * 4 + side], -1)

    up, down, left, right = [links[tau * 4 + side] for side in range(4)]
    tiles = [
        [up, look(left, 0), look(right, 0)],
        [tau, left, right],
        [down, look(left, 1), look(right, 1)],
    ]
    for padded in padded_all:
        padded[0:8, :] = jnp.zeros((8, 128), f32)
        padded[72:88, :] = jnp.zeros((16, 128), f32)
    for slot in range(4 * SLOTS):
        stage[slot * 16 + 8 : slot * 16 + 16, :] = jnp.zeros((8, 128), f32)
        if slot % SLOTS >= 51:
            stage[slot * 16 : slot * 16 + 8, :] = jnp.zeros((8, 128), f32)
    lane = lax.broadcasted_iota(jnp.int32, (56, 128), 1)
    for spot in range(32):
        source = early if spot < 28 else (late0 if spot < 30 else late1)
        at = (spot if spot < 28 else spot & 1) * PIECE + 544
        cells = source[at : at + 16, :].astype(f32)
        rows[spot : spot + 1, :] = cells[8:9].astype(jnp.int32)
    listing = pltpu.make_async_copy(rows, tabs, listed)
    listing.start()
    listing.wait()

    def put_line(hh, band, column, number):
        padded, shifted = padded_all[number % BUFFERS], shifted_all[number % BUFFERS]
        source = tiles[band][column]
        row = hh - 2 if band == 1 else (6 + hh if band == 0 else hh - 10)
        known = jnp.maximum(source, 0)
        spot, column_at = home(known), (known & 1) * 24 + row
        owner = tabs[spot, column_at]
        index = tabs[spot, column_at + 8]
        start = tabs[spot, column_at + 16] + 2
        usable = (source >= 0) & ((owner & 1) == core)
        cells = fetch(home(owner), index * LINE, LINE)
        padded[8 : 8 + LINE, :] = jnp.where(usable, cells, 0.0)
        first = (start >> 2) + 7
        turn = (start & 3) * 32
        lower = padded[pl.ds(first, 56), :]
        upper = padded[pl.ds(first + 1, 56), :]
        shifted[...] = pltpu.roll(jnp.where(lane >= turn, lower, upper), (128 - turn) & 127, 1)
        for dest in range(4):
            begin = ((view + dest) & 3) * 4
            if column == 0:
                stage[pl.ds(dest * PART + hh, 37, 16), :] = shifted[pl.ds(begin, 37), :]
            elif column == 1:
                stage[pl.ds(dest * PART + 37 * 16 + hh, 7, 16), :] = shifted[pl.ds(begin + 30, 7), :]
            else:
                stage[pl.ds(dest * PART + 44 * 16 + hh, 7, 16), :] = shifted[pl.ds(begin, 7), :]

    for hh in range(12):
        for column in range(3):
            put_line(hh, 0 if hh < 2 else (1 if hh < 10 else 2), column, hh * 3 + column)

    above = view < 2
    halo = [jnp.where(above, tiles[0][k], tiles[2][k]) for k in range(3)]
    halo_row = jnp.where(above, view, view + 8)

    def features(tile, extra, size):
        cells = fetch(home(jnp.maximum(tile, 0)), extra, size)
        return jnp.where((tile >= 0) & ((tile & 1) == core), cells, 0.0)

    cells = features(halo[0], 512, 32)
    for dest in range(4):
        stage[pl.ds(dest * PART + 12 + view, 32, 16), :] = cells

    def put_pair(cells, slot, row):
        for dest in range(4):
            for k in range(2):
                stage[pl.ds(dest * PART + (slot + k) * 16 + row, 1), :] = cells[k : k + 1]

    put_pair(features(halo[1], 528, 16)[14:16], 51, halo_row)
    put_pair(features(halo[2], 512, 16)[0:2], 53, halo_row)
    left_cells = features(left, 544, 16)
    right_cells = features(right, 544, 16)
    for k in range(2):
        put_pair(left_cells[4 * k + 2 : 4 * k + 4], 51, 2 + 2 * view + k)
        put_pair(right_cells[4 * k : 4 * k + 2], 53, 2 + 2 * view + k)

    out[...] = stage[...].astype(bf16)


def select_pieces(links, where_am_i, early, late):
    return pl.pallas_call(
        select_body,
        out_shape=jax.ShapeDtypeStruct((4 * PART, 128), bf16),
        in_specs=[pl.BlockSpec(memory_space=pltpu.SMEM)] * 2 + [pl.BlockSpec(memory_space=pltpu.VMEM)] * 3,
        out_specs=pl.BlockSpec(memory_space=pltpu.VMEM),
        scratch_shapes=[
            pltpu.VMEM((4 * PART, 128), f32),
            pltpu.VMEM((32, 128), jnp.int32),
            pltpu.SMEM((32, 128), jnp.int32),
            pltpu.SemaphoreType.DMA,
        ]
        + [pltpu.VMEM((88, 128), f32)] * BUFFERS
        + [pltpu.VMEM((56, 128), f32)] * BUFFERS,
        compiler_params=pltpu.CompilerParams(vmem_limit_bytes=12 << 20),
        name="select_pieces",
    )(links, where_am_i, *[near(x) for x in (early, *late)])


def slot_of(block, half):
    if block == 0:
        return 37 + half
    if block == BLOCKS - 1:
        return 44 + half
    return 2 * (block - 1) + half


def volume_body(
    facts, band0, band1, band2, band3, band4, ref, summing, first_bias, second_bias, first_far, second_far, out_far,
    turned, refx, factors, sums, padded, hidden0, hidden1, keep, wide, first, second, out, loaded, stored,
):
    first_copy = pltpu.make_async_copy(first_far, first, loaded.at[0])
    second_copy = pltpu.make_async_copy(second_far, second, loaded.at[1])
    first_copy.start()
    second_copy.start()
    view = facts[0]
    lane16 = lax.broadcasted_iota(jnp.int32, (16, 128), 1)
    sub8 = lax.broadcasted_iota(jnp.int32, (8, 128), 0)

    def total(slot):
        span = slice(slot * 16, slot * 16 + 16)
        if slot < HALF:
            opposite = band2[span, :].astype(f32)
        else:
            opposite = band4[slot * 16 - HALF * 16 : slot * 16 - HALF * 16 + 16, :].astype(f32)
        return (band0[span, :].astype(f32) + band1[span, :].astype(f32)) + (
            opposite + band3[span, :].astype(f32)
        )

    lanes = [lane16 >= 32 * m for m in range(4)]
    current = total(0)
    for slot in range(51):
        following = total(slot + 1)
        turned[slot] = current
        for m in range(1, 4):
            turned[m * 51 + slot] = pltpu.roll(
                jnp.where(lanes[m], current, following), 128 - 32 * m, 1
            )
        if slot < 32:
            block, half = 1 + slot // 2, slot % 2
            halo = pltpu.roll(current[8:16], 4, 0)
            own = pltpu.roll(ref[:, slot * 128 : slot * 128 + 128].astype(f32), 2, 0)
            refx[block * 2 + half, 0:8] = jnp.where(sub8 < 2, halo, own)
            refx[block * 2 + half, 8:16] = jnp.where(sub8 < 2, own, halo)
        current = following
    for half in range(2):
        refx[half] = total(51 + half)
        refx[2 * (BLOCKS - 1) + half] = total(53 + half)

    row = lax.broadcasted_iota(jnp.int32, (ROWS, 128), 0)
    high, block = row & 15, row >> 4
    inside = (high >= jnp.where(facts[1] >= 0, 0, 1)) & (high <= jnp.where(facts[2] >= 0, 9, 8))
    inside &= (block >= jnp.where(facts[3] >= 0, 0, 1))
    inside &= (block <= jnp.where(facts[4] >= 0, BLOCKS - 1, BLOCKS - 2))
    keep[...] = jnp.where(inside, 1.0, 0.0)
    sums[ROWS:, :] = jnp.zeros((sums.shape[0] - ROWS, 256), f32)
    hidden_two = (hidden0, hidden1)
    for hidden in hidden_two:
        hidden[ROWS:, :] = jnp.zeros((hidden.shape[0] - ROWS, 256), f32)

    def cost_step(q, carry):
        for m in range(4):
            dd = 4 * q + m
            for block in range(BLOCKS):
                for half in range(2):
                    product = refx[2 * block + half] * turned[m * 51 + slot_of(block, half) + q]
                    top = product.astype(bf16)
                    rest = (product - top.astype(f32)).astype(bf16)
                    at = block * 16
                    factors[half, at : at + 16, :] = top
                    factors[2 + half, at : at + 16, :] = rest
            cells = jnp.dot(
                jnp.concatenate([factors[k] for k in range(4)], axis=1), summing[...], preferred_element_type=f32
            )
            depth = 16 * view + dd - 2
            sums[0:ROWS, :] = jnp.where((depth >= 0) & (depth < NDISP), cells, 0.0)
            from_right = (lane16 & 8) == 8

            def mixed_cells(block):
                low = [sums[block * 16 + b : block * 16 + b + 16, 128:256] for b in range(3)]
                return low[2], jnp.where(lane16 >= 96, low[2], jnp.where(lane16 >= 80, low[1], low[0]))

            this_low, this_mixed = mixed_cells(0)
            last_mixed = this_mixed
            for block in range(BLOCKS):
                at = block * 16
                next_low, next_mixed = mixed_cells(min(block + 1, BLOCKS - 1))
                head = jnp.where(lane16 < 64, sums[at : at + 16, 0:128], sums[at + 1 : at + 17, 0:128])
                edge = jnp.where(from_right, next_mixed, last_mixed)
                tail = jnp.where(lane16 < 64, this_low, edge)
                line = pl.multiple_of(dd * ROWS + at, 16)
                padded[0, pl.ds(line, 16), :] = head.astype(bf16)
                padded[1, pl.ds(line, 16), :] = tail.astype(bf16)
                this_low, last_mixed, this_mixed = next_low, this_mixed, next_mixed
        return carry

    lax.fori_loop(0, 5, cost_step, 0)

    lane8 = lax.broadcasted_iota(jnp.int32, (8, 128), 1)

    def hidden_cells(step, hidden):
        cells = jnp.broadcast_to(first_bias[...], (ROWS, 256))
        for a in range(3):
            at = pl.multiple_of((step + a) * ROWS, 16)
            cells = cells + jnp.dot(
                jnp.concatenate([padded[k, pl.ds(at, ROWS), :] for k in range(2)], axis=1),
                first[a],
                preferred_element_type=f32,
            )
        depth = 16 * view + step - 1
        live = jnp.where((depth >= 0) & (depth < NDISP), keep[...], 0.0) > 0.5
        for part in range(2):
            span = slice(part * 128, part * 128 + 128)
            hidden[0:ROWS, span] = jnp.where(live, jnp.maximum(cells[:, span], 0.0), 0.0)

        def block_cells(block):
            at = block * 16
            parts, edges = [], []
            for b in range(3):
                parts.append(hidden[at + b : at + b + 8, 0:128])
                parts.append(hidden[at + b : at + b + 8, 128:256])
                before = hidden[at + b - 16 : at + b - 8, 128:256]
                after = hidden[at + b + 16 : at + b + 24, 0:128]
                edges.append(pltpu.roll(jnp.where(lane8 < 96, after, before), 96 if b == 1 else 32, 1))
            parts.append(jnp.where(lane8 < 64, edges[0], edges[1]))
            parts.append(edges[2])
            return parts

        for pair in range(8):
            one = block_cells(1 + 2 * pair)
            two = block_cells(2 + 2 * pair)
            at = pl.multiple_of(step * 128 + pair * 16, 16)
            for part in range(8):
                wide[part, pl.ds(at, 16), :] = jnp.concatenate(
                    [one[part], two[part]], axis=0
                ).astype(bf16)

    def hidden_step(pair, carry):
        for k in range(2):
            hidden_cells(pair * 2 + k, hidden_two[k])
        return carry

    first_copy.wait()
    lax.fori_loop(0, DL // 2 + 1, hidden_step, 0)
    second_copy.wait()

    def stores(step):
        span = pl.ds(step * 4, 4)
        return pltpu.make_async_copy(out.at[span], out_far.at[span], stored.at[step])

    def output_step(step, carry):
        cells = jnp.broadcast_to(second_bias[...], (512, 256))
        for a in range(3):
            at = pl.multiple_of((step * 4 + a) * 128, 128)
            cells = cells + jnp.dot(
                jnp.concatenate([wide[k, pl.ds(at, 512), :] for k in range(8)], axis=1),
                second[a],
                preferred_element_type=f32,
            )
        for d in range(4):
            for block in range(16):
                at = d * 128 + block * 8
                out[step * 4 + d, :, block * 256 : block * 256 + 256] = cells[at : at + 8, :]
        stores(step).start()
        return carry

    lax.fori_loop(0, 4, output_step, 0)
    for step in range(4):
        stores(step).wait()


def volume(facts, bands, ref, first, first_bias, second, second_bias):
    operands = (
        facts, *[near(band) for band in bands], ref, jnp.asarray(group_sum_matrix(), bf16),
        first_bias, second_bias,
    )
    return pl.pallas_call(
        volume_body,
        out_shape=jax.ShapeDtypeStruct((DL, H, W * CH), f32),
        in_specs=[pl.BlockSpec(memory_space=pltpu.SMEM)]
        + [pl.BlockSpec(memory_space=pltpu.VMEM)] * 9
        + [pl.BlockSpec(memory_space=pl.ANY)] * 2,
        out_specs=pl.BlockSpec(memory_space=pl.ANY),
        scratch_shapes=[
            pltpu.VMEM((4 * 51, 16, 128), f32),
            pltpu.VMEM((2 * BLOCKS, 16, 128), f32),
            pltpu.VMEM((4, ROWS, 128), bf16),
            pltpu.VMEM((ROWS + 16, 256), f32),
            pltpu.VMEM((2, 20 * ROWS, 128), bf16),
            pltpu.VMEM((ROWS + 16, 256), f32),
            pltpu.VMEM((ROWS + 16, 256), f32),
            pltpu.VMEM((ROWS, 128), f32),
            pltpu.VMEM((8, 18 * 128, 128), bf16),
            pltpu.VMEM(first.shape, bf16),
            pltpu.VMEM(second.shape, bf16),
            pltpu.VMEM((DL, H, W * CH), f32),
            pltpu.SemaphoreType.DMA((2,)),
            pltpu.SemaphoreType.DMA((4,)),
        ],
        compiler_params=pltpu.CompilerParams(vmem_limit_bytes=48 << 20),
        name="volume",
    )(*operands, first, second)


def on_device(
    ref_features, partner_lines, line_owner, line_index, line_offset, neighbours,
    conv1_weight, conv1_bias, conv2_weight, conv2_bias,
):
    view = lax.axis_index("views")
    core = lax.axis_index("c")
    tile = (lax.axis_index("z") * XB + lax.axis_index("x")) * CB + core
    ref = ref_features[0]

    lines = lax.dynamic_index_in_dim(partner_lines[0], view, 0, keepdims=False)
    halo_row = lax.dynamic_slice_in_dim(ref, (view + 6) % 8, 1, axis=0)
    sides = lax.dynamic_slice_in_dim(ref, 2 * view, 2, axis=0)
    sides = jnp.concatenate([sides[:, 0:256], sides[:, 3840:4096]], axis=1)
    names = jnp.stack([line_owner[0, :, 0], line_index[0], line_offset[0]])
    names = lax.dynamic_slice_in_dim(names, view * 8, 8, axis=1).astype(bf16).reshape(24)
    twin = lax.ppermute(names, "c", [(0, 1), (1, 0)])
    names = jnp.where(core == 0, jnp.concatenate([names, twin]), jnp.concatenate([twin, names]))
    payload = jnp.concatenate(
        [
            lines.reshape(8 * LINE, 128),
            halo_row.reshape(32, 128),
            sides.reshape(8, 128),
            jnp.pad(names[None], ((0, 7), (0, 80))),
        ],
        axis=0,
    )

    def shift(x, axis, by):
        count = lax.axis_size(axis)
        return lax.ppermute(x, axis, [(i, (i + by) % count) for i in range(count)])

    one, two, three = shift(payload, "x", 1), shift(payload, "x", -1), shift(payload, "x", 2)
    chunks = [[None, None] for _ in range(8)]
    chunks[0] = [jnp.concatenate([payload, one]), jnp.concatenate([two, three])]
    for k in range(1, 4):
        for i in range(2):
            chunks[-k % 8][i] = shift(chunks[(1 - k) % 8][i], "z", 1)
            chunks[k][i] = shift(chunks[k - 1][i], "z", -1)
    last = [shift(chunks[5][0], "z", 1), shift(chunks[3][1], "z", -1)]
    early = merge_chunks([chunk for k in range(8) if k != 4 for chunk in chunks[k]])

    links = neighbours.reshape(256)

    first, second = spread_weights(conv1_weight, conv2_weight)
    first_bias = jnp.tile(conv1_bias, 8)[None]
    second_bias = jnp.tile(conv2_bias, 8)[None]
    facts = jnp.concatenate([view[None], neighbours[tile]])
    other = tile + 1 - 2 * core
    asked = jnp.stack([other, core, view, tile])
    wanted = jnp.stack([tile, core, view, tile])
    links, asked, wanted, first, second, first_bias, second_bias, facts = lax.optimization_barrier(
        (links, asked, wanted, first, second, first_bias, second_bias, facts)
    )
    theirs = select_pieces(links, asked, early, last)
    swapped = lax.ppermute(theirs, "c", [(0, 1), (1, 0)])
    own = select_pieces(links, wanted, early, last)

    def part(begin, end):
        return own[begin:end] + swapped[begin:end]

    middle = 2 * PART + HALF * 16
    upward = shift(part(2 * PART, middle), "views", 1)
    downward = shift(part(middle, 3 * PART), "views", -1)
    bands = [
        part(0, PART),
        shift(part(PART, 2 * PART), "views", 1),
        shift(upward, "views", 1),
        shift(part(3 * PART, 4 * PART), "views", -1),
        shift(downward, "views", -1),
    ]
    return volume(facts, bands, ref, first, first_bias, second, second_bias)[None]


def solution(mesh):
    fine = Mesh(mesh.devices.reshape(ZB, XB, CB, NPV), ("z", "x", "c", "views"))
    tiles = ("z", "x", "c")
    return jax.shard_map(
        on_device,
        mesh=fine,
        in_specs=(
            P(tiles, None, None),
            P(tiles, None, None, None),
            P(tiles, None, None),
            P(tiles, None),
            P(tiles, None),
            P(),
            P(),
            P(),
            P(),
            P(),
        ),
        out_specs=P(tiles, "views", None, None),
        check_vma=False,
    )
```
